256 devices in a mesh: sec: 2 (over y_lo), gz: 128 (over x, z, y_hi, core).
Axes of the slice: x: 4, y: 4 (y_hi: 2, y_lo: 2; y = y_hi * 2 + y_lo), z: 8, core: 2. Of those that a mesh axis runs over, the one named last changes fastest.
Arguments:
- velocity: float32 [2, 3, 256, 512, 256], P('sec', None, 'gz'), may hold values from -6 to 6
- eddy_viscosity: float32 [2, 256, 512, 256], P('sec', 'gz'), may hold values from 0.05 to 0.5
- turbine_mask: int32 [256, 512, 256], P('gz'), may hold values 0 or 1
- fringe_columns: int32 [64], replicated, may hold values from 0 to 511, as said below
Outputs:
- new_velocity: float32 [2, 3, 256, 512, 256], P('sec', None, 'gz')
The draws below stay inside these ranges and needn't reach their ends.
Inputs may be any that keep to these rules, and one draw needn't show every extreme that they name: `fringe_columns`: 64 distinct streamwise column indices.
All inputs are finite; a program needn't handle non-finite values. No bound on the sum of `turbine_mask` on one device may be relied on, other than what follows from the above.
Results may differ from the reference program's by a relative error of at most 0.0003.
Values sent between devices are 32-bit elements; how exact they have to be, the bound alone decides.
A program may use at most 128 MiB of HBM per device.

```python
import math
import jax
import jax.numpy as jnp
from jax import lax

NX = 512
NY = 256
NF = 64
NZ = 256
N_SEC = 2


def draw_fringe_columns(key, part):
    return jax.random.permutation(key, NX)[:NF].astype(jnp.int32)


def with_ends(drawn, rng, least, top_value):
    place = [jax.random.randint(jax.random.fold_in(rng, axis), (), 0, length) for axis, length in enumerate(drawn.shape)]
    widest = drawn.shape.index(max(drawn.shape))
    next_to = place[:widest] + [(place[widest] + 1) % drawn.shape[widest]] + place[widest + 1:]
    return drawn.at[tuple(place)].set(least).at[tuple(next_to)].set(top_value)


def shard_levels(stream_key, dims, split, low, high):
    gain, own = 1.0, jax.random.fold_in(stream_key, 6)
    for dim, parts in split:
        draws = jnp.exp(jax.random.uniform(jax.random.fold_in(own, dim), (parts,), jnp.float32, low / len(split), high / len(split)))
        gain = gain * jnp.repeat(draws, dims[dim] // parts).reshape([-1 if axis == dim else 1 for axis in range(len(dims))])
    return gain


def noise(rng, dims, scale, reach, split=(), held_as=jnp.bfloat16):
    entries = scale * jax.random.normal(rng, dims, jnp.float32)
    if split:
        entries = entries * shard_levels(rng, dims, split, -0.22, 0.18)
    return jnp.clip(entries, -reach, reach).astype(held_as)


def setup_inputs(seed: int = 0) -> dict:
    splits = jax.random.split(jax.random.key(seed), 5)
    velocity = noise(splits[0], (N_SEC, 3, NZ, NX, NY), 1.0, 6.0, ((0, 2), (2, 128)), jnp.float32)
    eddy_viscosity = jnp.clip(jnp.exp(math.log(0.5) - 2.3025851 * jax.random.uniform(splits[1], (N_SEC, NZ, NX, NY), jnp.float32) ** shard_levels(splits[1], (N_SEC, NZ, NX, NY), ((0, 2), (1, 128)), -0.2, 0.2)), 0.05, 0.5)
    turbine_mask = with_ends((jax.random.randint(splits[2], (NZ, NX, NY), 0, 16) < 1).astype(jnp.int32), jax.random.fold_in(splits[2], 1), 0, 1)
    fringe_columns = draw_fringe_columns(jax.random.fold_in(splits[4], 71), 0)
    return {"velocity": velocity, "eddy_viscosity": eddy_viscosity, "turbine_mask": turbine_mask, "fringe_columns": fringe_columns}


step_size = 0.1
drag_coef = 0.75
cell_width = 4.0
highest = lax.Precision.HIGHEST

def derivative_table(length, cutoff):
    position = jnp.arange(length, dtype=jnp.int32)
    wavenumber = jnp.arange(1, cutoff + 1, dtype=jnp.int32)
    phases = position[:, None] * wavenumber[None, :] % length
    angles = 2.0 * math.pi / length * phases.astype(jnp.float32)
    sine_table = jnp.sin(angles)
    cosines = jnp.cos(angles)
    weight = (4.0 * math.pi / (length * length * cell_width) * wavenumber.astype(jnp.float32))[None, :]
    return jnp.dot(cosines * weight, sine_table.T, precision=highest) - jnp.dot(sine_table * weight, cosines.T, precision=highest)

def real_basis(length):
    midpoint = length // 2
    row_index = jnp.arange(length, dtype=jnp.int32)
    position = jnp.arange(length, dtype=jnp.int32)
    wavenumber = jnp.where(row_index <= midpoint, row_index, row_index - midpoint)
    phases = wavenumber[:, None] * position[None, :] % length
    angles = 2.0 * math.pi / length * phases.astype(jnp.float32)
    scales = jnp.where((row_index == 0) | (row_index == midpoint), math.sqrt(1.0 / length), math.sqrt(2.0 / length)).astype(jnp.float32)
    shapes = jnp.where((row_index <= midpoint)[:, None], jnp.cos(angles), jnp.sin(angles))
    return scales[:, None] * shapes

def wave_square(row_index, length):
    midpoint = length // 2
    wavenumber = jnp.where(row_index < midpoint, row_index, jnp.where(row_index == midpoint, 0, row_index - midpoint))
    scaled = 2.0 * math.pi / (length * cell_width) * wavenumber.astype(jnp.float32)
    return -(scaled * scaled)

def cosine_basis(length):
    mode_index = jnp.arange(length, dtype=jnp.int32)
    position = jnp.arange(length, dtype=jnp.int32)
    phases = mode_index[:, None] * (2 * position[None, :] + 1) % (4 * length)
    angles = math.pi / (2 * length) * phases.astype(jnp.float32)
    scales = jnp.where(mode_index == 0, math.sqrt(1.0 / length), math.sqrt(2.0 / length)).astype(jnp.float32)
    return scales[:, None] * jnp.cos(angles)

def vertical_eigen(mode_index, length):
    sines = jnp.sin(math.pi / (2 * length) * mode_index.astype(jnp.float32))
    return -4.0 * sines * sines

def column_inverse(height, length_x, length_y, first_column, column_count):
    mode_index = jnp.arange(height, dtype=jnp.int32)
    column = first_column + jnp.arange(column_count, dtype=jnp.int32)
    row_x = column // length_y
    row_y = column % length_y
    eigenvalue = vertical_eigen(mode_index, height)[:, None] + wave_square(row_x, length_x)[None, :] + wave_square(row_y, length_y)[None, :]
    null_x = (row_x == 0) | (row_x == length_x // 2)
    null_y = (row_y == 0) | (row_y == length_y // 2)
    null_mode = (mode_index == 0)[:, None] & (null_x & null_y)[None, :]
    return jnp.where(null_mode, 0.0, 1.0 / jnp.where(null_mode, -1.0, eigenvalue))

def tendency(current, viscosity, drag_field, dealias_x, dealias_y):
    rounded = lax.optimization_barrier(current.astype(jnp.bfloat16)).astype(jnp.float32)
    grad_x = jnp.einsum('ij,czjy->cziy', dealias_x, rounded)
    grad_y = jnp.einsum('czxj,ij->czxi', rounded, dealias_y)
    padded = jnp.pad(current, ((0, 0), (1, 1), (0, 0), (0, 0)))
    upper_plane = padded[:, 2:]
    lower_plane = padded[:, :-2]
    grad_z = 0.5 * (upper_plane - lower_plane)
    laplace = upper_plane - 2.0 * current + lower_plane
    advection = -(current[0] * grad_x + current[1] * grad_y + current[2] * grad_z)
    return advection + viscosity * laplace - drag_field * jnp.abs(current[0]) * current

def project(current, full_x, full_y, basis_x, basis_y, basis_z, inverse):
    height = current.shape[1]
    length_x = current.shape[2]
    length_y = current.shape[3]
    at_lid = (jnp.arange(height, dtype=jnp.int32) == height - 1)[:, None, None]
    w_face = jnp.where(at_lid, 0.0, current[2])
    beneath = jnp.pad(w_face, ((1, 0), (0, 0), (0, 0)))[:-1]
    divergence = jnp.einsum('ij,zjy->ziy', full_x, current[0], precision=highest) + jnp.einsum('zxj,ij->zxi', current[1], full_y, precision=highest)
    source = divergence + w_face - beneath
    partial_value = jnp.einsum('ax,zxy->zay', basis_x, source, precision=highest)
    spectra = jnp.einsum('zay,by->zab', partial_value, basis_y, precision=highest).reshape(height, length_x * length_y)
    solved = jnp.dot(basis_z, spectra, precision=highest) * inverse
    solved = jnp.dot(basis_z.T, solved, precision=highest).reshape(height, length_x, length_y)
    partial_value = jnp.einsum('ax,zab->zxb', basis_x, solved, precision=highest)
    pressure = jnp.einsum('zxb,by->zxy', partial_value, basis_y, precision=highest)
    overhead = jnp.pad(pressure, ((0, 1), (0, 0), (0, 0)))[1:]
    lift = jnp.where(at_lid, 0.0, overhead - pressure)
    new_u = current[0] - jnp.einsum('ij,zjy->ziy', full_x, pressure, precision=highest)
    new_v = current[1] - jnp.einsum('zxj,ij->zxi', pressure, full_y, precision=highest)
    return jnp.stack([new_u, new_v, w_face - lift])

def reference(velocity, eddy_viscosity, turbine_mask, fringe_columns):
    height = velocity.shape[2]
    length_x = velocity.shape[3]
    length_y = velocity.shape[4]
    dealias_x = lax.optimization_barrier(derivative_table(length_x, (length_x - 1) // 3).astype(jnp.bfloat16)).astype(jnp.float32)
    dealias_y = lax.optimization_barrier(derivative_table(length_y, (length_y - 1) // 3).astype(jnp.bfloat16)).astype(jnp.float32)
    full_x = derivative_table(length_x, length_x // 2 - 1)
    full_y = derivative_table(length_y, length_y // 2 - 1)
    basis_x = real_basis(length_x)
    basis_y = real_basis(length_y)
    basis_z = cosine_basis(height)
    inverse = column_inverse(height, length_x, length_y, jnp.int32(0), length_x * length_y)
    farm_drag = drag_coef * turbine_mask.astype(jnp.float32)
    tables = (full_x, full_y, basis_x, basis_y, basis_z, inverse)

    def inflow(precursor, farm):
        return farm.at[:, :, fringe_columns, :].set(precursor[:, :, fringe_columns, :])
    precursor_start = velocity[0]
    farm_start = inflow(velocity[0], velocity[1])
    precursor_mid = project(precursor_start + step_size * tendency(precursor_start, eddy_viscosity[0], 0.0, dealias_x, dealias_y), *tables)
    farm_mid = project(farm_start + step_size * tendency(farm_start, eddy_viscosity[1], farm_drag, dealias_x, dealias_y), *tables)
    farm_mid = inflow(precursor_mid, farm_mid)
    precursor_end = project(0.5 * (precursor_start + precursor_mid + step_size * tendency(precursor_mid, eddy_viscosity[0], 0.0, dealias_x, dealias_y)), *tables)
    farm_end = project(0.5 * (farm_start + farm_mid + step_size * tendency(farm_mid, eddy_viscosity[1], farm_drag, dealias_x, dealias_y)), *tables)
    return jnp.stack([precursor_end, farm_end])
```

```python
import functools
import math

import jax
import jax.numpy as jnp
import numpy as np
from jax import lax
from jax.experimental import pallas as pl
from jax.experimental.pallas import tpu as pltpu
from jax.sharding import PartitionSpec as P

step_size = 0.1
drag_coef = 0.75
cell_width = 4.0
f32 = jnp.float32
bf16 = jnp.bfloat16
MIB = 1024 * 1024


def derivative_np(n, cutoff):
    i = np.arange(n)
    k = np.arange(1, cutoff + 1)
    wave = 2.0 * np.pi * k / n
    shift = np.sin(2.0 * np.pi / n * ((i[:, None] * k[None, :]) % n)) @ wave
    shift = -(2.0 / (cell_width * n)) * shift
    return shift[(i[:, None] - i[None, :]) % n]


def basis_np(n):
    mid = n // 2
    r = np.arange(n)
    k = np.where(r <= mid, r, r - mid)
    angle = 2.0 * np.pi / n * ((k[:, None] * r[None, :]) % n)
    scale = np.where((r == 0) | (r == mid), math.sqrt(1.0 / n), math.sqrt(2.0 / n))
    return scale[:, None] * np.where((r <= mid)[:, None], np.cos(angle), np.sin(angle))


def basis_slope_np(n):
    slope = basis_np(n) @ derivative_np(n, n // 2 - 1)
    slope[0] = 0.0
    slope[n // 2] = 0.0
    return slope


def hi_lo(table):
    table = np.asarray(table, np.float32)
    hi = table.astype(bf16)
    lo = (table - hi.astype(np.float32)).astype(bf16)
    return np.stack([hi, lo])


def dot(a, b):
    return jnp.dot(a, b, preferred_element_type=f32)


def split(x):
    hi = x.astype(bf16)
    return hi, (x - hi.astype(f32)).astype(bf16)


def left3(t_ref, x):
    hi, lo = split(x)
    return dot(t_ref[0], hi) + (dot(t_ref[1], hi) + dot(t_ref[0], lo))


def right3(x, t_ref):
    hi, lo = split(x)
    return dot(hi, t_ref[0]) + (dot(hi, t_ref[1]) + dot(lo, t_ref[0]))


def wave_gap(row, length):
    mid = length // 2
    k = jnp.where(row < mid, row, jnp.where(row == mid, 0, row - mid)).astype(f32)
    scaled = (2.0 * math.pi / (length * cell_width)) * k
    return scaled * scaled


def tile_gap(first_a, first_b, rows, lanes, nx, ny):
    a = first_a + lax.broadcasted_iota(jnp.int32, (rows, lanes), 0)
    b = first_b + lax.broadcasted_iota(jnp.int32, (rows, lanes), 1)
    return wave_gap(a, nx) + wave_gap(b, ny)


def interior_inverse(mu, is_last):
    det = mu * (mu * mu - 2.0)
    lid = mu * mu * (mu - 1.0) - 2.0 * mu + 1.0
    recip = 1.0 / jnp.where(is_last, lid, det)
    m1 = mu - 1.0
    q11 = jnp.where(is_last, mu * m1 - 1.0, mu * mu - 1.0) * recip
    q12 = jnp.where(is_last, m1, mu) * recip
    q13 = recip
    q22 = jnp.where(is_last, mu * m1, mu * mu) * recip
    q23 = mu * recip
    q33 = (mu * mu - 1.0) * recip
    return q11, q12, q13, q22, q23, q33


def pack_kernel(idx_ref, v_ref, lev0, lev1, fr, fr0, fr1):
    for c in range(3):
        lev0[c] = v_ref[c, 0]
        lev1[c] = v_ref[c, 1]
    pack_rows(idx_ref, (lev0, lev1), fr, fr0, fr1)


def pack_rows(idx_ref, levels, fr, fr0, fr1):
    def body(f, carry):
        row = idx_ref[f]
        for c in range(3):
            low = levels[0][c, pl.ds(row, 1), :]
            high = levels[1][c, pl.ds(row, 1), :]
            fr[0, c, pl.ds(f, 1), :] = low
            fr[1, c, pl.ds(f, 1), :] = high
            fr0[c, pl.ds(f, 1), :] = low
            fr1[c, pl.ds(f, 1), :] = high
        return carry

    lax.fori_loop(0, idx_ref.shape[0], body, 0)


def put_rows(idx_ref, target, source):
    def body(f, carry):
        row = idx_ref[f]
        for c in range(3):
            target[c, pl.ds(row, 1), :] = source[c, pl.ds(f, 1), :]
        return carry

    lax.fori_loop(0, idx_ref.shape[0], body, 0)


def advect_kernel(idx_ref, lev0, lev1, fr, mask, dlx, dly, part, state):
    is_farm = lax.axis_index("sec") == 1
    state[0] = lev0[...]
    state[1] = lev1[...]

    @pl.when(is_farm)
    def _():
        put_rows(idx_ref, state.at[0], fr.at[0])
        put_rows(idx_ref, state.at[1], fr.at[1])

    coef = jnp.where(is_farm, drag_coef, 0.0).astype(f32)
    for z in range(2):
        u = state[z, 0]
        v = state[z, 1]
        drag = coef * mask[z].astype(f32) * jnp.abs(u)
        for c in range(3):
            here = state[z, c]
            r = here.astype(bf16)
            gx = dot(dlx[...], r)
            gy = dot(r, dly[...])
            part[z, c] = -(u * gx + v * gy) - drag * here


def forward_kernel(second, *refs):
    refs = list(refs)
    idx_ref, lev0, lev1, fr, halo_lo, halo_hi, fr_lo, fr_hi, part, visc = refs[:10]
    refs = refs[10:]
    if second:
        old0, old1, old_fr = refs[:3]
        refs = refs[3:]
    by, byd, bx, bxd, vout, keep, send, state, halo, spec = refs[:10]
    if second:
        old = refs[10]
    nx = lev0.shape[1]
    is_farm = lax.axis_index("sec") == 1
    me = lax.axis_index("gz")
    core = lax.rem(me, 2)
    not_lid = (me != lax.axis_size("gz") - 1).astype(f32)
    state[0] = lev0[...]
    state[1] = lev1[...]
    halo[0] = halo_lo[...]
    halo[1] = halo_hi[...]
    if second:
        old[0] = old0[...]
        old[1] = old1[...]

    @pl.when(is_farm)
    def _():
        put_rows(idx_ref, state.at[0], fr.at[0])
        put_rows(idx_ref, state.at[1], fr.at[1])
        put_rows(idx_ref, halo.at[0], fr_lo)
        put_rows(idx_ref, halo.at[1], fr_hi)
        if second:
            put_rows(idx_ref, old.at[0], old_fr.at[0])
            put_rows(idx_ref, old.at[1], old_fr.at[1])

    for z in range(2):
        for c in range(3):
            here = state[z, c]
            below = halo[0, c] if z == 0 else state[0, c]
            above = state[1, c] if z == 0 else halo[1, c]
            tend = part[z, c] - state[z, 2] * (0.5 * (above - below))
            tend = tend + visc[z] * (above - 2.0 * here + below)
            if second:
                new = 0.5 * (old[z, c] + here + step_size * tend)
            else:
                new = here + step_size * tend
            if z == 1 and c == 2:
                new = new * not_lid
            vout[z, c] = new
    w0 = right3(vout[0, 2], by)
    w1 = right3(vout[1, 2], by)
    g0 = right3(vout[0, 1], byd) + w0
    g1 = right3(vout[1, 1], byd) + (w1 - w0)
    spec[0] = left3(bxd, right3(vout[0, 0], by)) + left3(bx, g0)
    spec[1] = left3(bxd, right3(vout[1, 0], by)) + left3(bx, g1)
    spec[2] = left3(bx, w1)
    half = nx // 2
    keep[...] = spec[:, pl.ds(pl.multiple_of(core * half, half), half), :]
    send[...] = spec[:, pl.ds(pl.multiple_of((1 - core) * half, half), half), :]


def sources(core, keep, recv, rows):
    first = core == 0

    def pick(field, low):
        own, other = keep[field, rows, :], recv[field, rows, :]
        return jnp.where(first == low, own, other)

    s1 = pick(1, True)
    s2 = pick(0, False) - pick(2, True)
    s3 = pick(1, False)
    return pick, s1, s2, s3


def reduce_kernel(nx, ny, chips, keep, recv, out):
    me = lax.axis_index("gz")
    core = lax.rem(me, 2)
    is_last = lax.div(me, 2) == chips - 1
    half = keep.shape[1]
    lane_blocks = ny // 128

    def body(rb, carry):
        rows = pl.ds(pl.multiple_of(rb * 8, 8), 8)
        pick, s1, s2, s3 = sources(core, keep, recv, rows)
        mu = 2.0 + tile_gap(core * half + rb * 8, 0, 8, ny, nx, ny)
        q11, q12, q13, q22, q23, q33 = interior_inverse(mu, is_last)
        a = -pick(0, True) - (q11 * s1 + q12 * s2 + q13 * s3)
        c = pick(2, False) - (q13 * s1 + q23 * s2 + q33 * s3)
        for lb in range(lane_blocks):
            out[rb * lane_blocks + lb, 0] = a[:, lb * 128 : (lb + 1) * 128]
            out[rb * lane_blocks + lb, 1] = c[:, lb * 128 : (lb + 1) * 128]
        return carry

    lax.fori_loop(0, half // 8, body, 0)


def own_gap(nx, ny):
    me = lax.axis_index("gz")
    core = lax.rem(me, 2)
    chip = lax.div(me, 2)
    lane_blocks = ny // 128
    first_a = core * (nx // 2) + lax.div(chip, lane_blocks) * 8
    first_b = lax.rem(chip, lane_blocks) * 128
    return tile_gap(first_a, first_b, 8, 128, nx, ny)


def pivot_kernel(nx, ny, chips, pivots):
    eps = own_gap(nx, ny)
    mu = 2.0 + eps
    mm = mu * mu
    inner = mm * eps * (4.0 + eps)
    lid = mm * (mu - 1.0) - 2.0 * mu + 1.0
    last = mu * eps * (mm * mm * (mu + 1.0) - mm * (4.0 * mu + 3.0) + 3.0 * mu + 1.0) / lid
    e = mu * eps * (mm + mu - 1.0)
    pivot = 1.0 / (1.0 + e)
    pivots[0] = pivot

    def body(j, carry):
        e, pivot = carry
        e = inner + e * pivot
        pivot = 1.0 / (1.0 + e)
        pivots[j] = pivot
        return e, pivot

    e, pivot = lax.fori_loop(1, chips - 1, body, (e, pivot))
    e = last + e * pivot
    pivots[chips - 1] = jnp.where(e > 0.0, 1.0 / jnp.where(e > 0.0, e, 1.0), 0.0)


def column_kernel(nx, ny, chips, pivots, x, out, work):
    mu = 2.0 + own_gap(nx, ny)
    det = mu * (mu * mu - 2.0)
    y = det * x[0, 0] * pivots[0]
    work[0] = y
    for j in range(1, chips):
        y = (det * (x[j, 0] + x[j - 1, 1]) + y) * pivots[j]
        work[j] = y
    out[chips - 1, 0] = y
    out[chips - 1, 1] = jnp.zeros_like(y)
    for j in range(chips - 2, -1, -1):
        out[j, 1] = y
        y = work[j] + y * pivots[j]
        out[j, 0] = y


def expand_kernel(nx, ny, chips, keep, recv, x, own, send):
    me = lax.axis_index("gz")
    core = lax.rem(me, 2)
    is_last = lax.div(me, 2) == chips - 1
    half = keep.shape[1]
    lane_blocks = ny // 128

    def body(rb, carry):
        rows = pl.ds(pl.multiple_of(rb * 8, 8), 8)
        _, s1, s2, s3 = sources(core, keep, recv, rows)
        mu = 2.0 + tile_gap(core * half + rb * 8, 0, 8, ny, nx, ny)
        q11, q12, q13, q22, q23, q33 = interior_inverse(mu, is_last)
        p0 = jnp.concatenate([x[rb * lane_blocks + lb, 0] for lb in range(lane_blocks)], axis=1)
        p4 = jnp.concatenate([x[rb * lane_blocks + lb, 1] for lb in range(lane_blocks)], axis=1)
        s1 = s1 - p0
        s3 = s3 - p4
        p1 = -(q11 * s1 + q12 * s2 + q13 * s3)
        p2 = -(q12 * s1 + q22 * s2 + q23 * s3)
        p3 = -(q13 * s1 + q23 * s2 + q33 * s3)
        p4 = jnp.where(is_last, p3, p4)
        first = core == 0
        for field, (low, high) in enumerate(((p0, p2), (p1, p3), (p2, p4))):
            own[field, rows, :] = jnp.where(first, low, high)
            send[field, rows, :] = jnp.where(first, high, low)
        return carry

    lax.fori_loop(0, half // 8, body, 0)


def backward_kernel(final, *refs):
    refs = list(refs)
    if not final:
        idx_ref = refs.pop(0)
    own, recv, vin, by, byd, bx, bxd = refs[:7]
    outs = refs[7:-1]
    press = refs[-1]
    half = own.shape[1]
    core = lax.rem(lax.axis_index("gz"), 2)
    press[:, pl.ds(pl.multiple_of(core * half, half), half), :] = own[...]
    press[:, pl.ds(pl.multiple_of((1 - core) * half, half), half), :] = recv[...]
    for z in range(2):
        p = press[z]
        lift = press[z + 1] - p
        new_u = vin[z, 0] - right3(left3(bxd, p), by)
        new_v = vin[z, 1] - right3(left3(bx, p), byd)
        new_w = vin[z, 2] - right3(left3(bx, lift), by)
        for c, new in enumerate((new_u, new_v, new_w)):
            if final:
                outs[0][c, z] = new
            else:
                outs[z][c] = new
    if not final:
        pack_rows(idx_ref, outs[:2], *outs[2:])


VM = pl.BlockSpec(memory_space=pltpu.VMEM)
SM = pl.BlockSpec(memory_space=pltpu.SMEM)


def shape(*dims):
    return jax.ShapeDtypeStruct(dims, f32)


def call(kernel, ins, outs, scratch=(), smem=0, limit=40, flops=0):
    many = isinstance(outs, (list, tuple))
    moved = sum(x.size * x.dtype.itemsize for x in ins)
    moved += sum(math.prod(o.shape) * 4 for o in (outs if many else [outs]))
    return pl.pallas_call(
        kernel,
        out_shape=outs,
        in_specs=[SM] * smem + [VM] * (len(ins) - smem),
        out_specs=[VM] * len(outs) if many else VM,
        scratch_shapes=[pltpu.VMEM(s, f32) for s in scratch],
        compiler_params=pltpu.CompilerParams(vmem_limit_bytes=limit * MIB),
        cost_estimate=pl.CostEstimate(flops=flops, bytes_accessed=moved, transcendentals=0),
    )(*ins)


def local(velocity, eddy_viscosity, turbine_mask, idx):
    velocity = velocity[0]
    visc = eddy_viscosity[0]
    _, _, nx, ny = velocity.shape
    fringe = idx.shape[0]
    slabs = lax.axis_size("gz")
    chips = slabs // 2
    half = nx // 2
    plane = 2 * nx * ny

    slope_x, slope_y = basis_slope_np(nx), basis_slope_np(ny)
    base_x, base_y = basis_np(nx), basis_np(ny)
    dlx = jnp.asarray(derivative_np(nx, (nx - 1) // 3).astype(np.float32).astype(bf16))
    dly = jnp.asarray(derivative_np(ny, (ny - 1) // 3).T.astype(np.float32).astype(bf16))
    fore = tuple(jnp.asarray(hi_lo(t)) for t in (base_y.T, slope_y.T, base_x, slope_x))
    back = tuple(jnp.asarray(hi_lo(t)) for t in (base_y, -slope_y, base_x.T, -slope_x.T))

    up = [(i, i + 1) for i in range(slabs - 1)]
    down = [(i + 1, i) for i in range(slabs - 1)]
    swap = [(i, i ^ 1) for i in range(slabs)]
    groups = [list(range(c, slabs, 2)) for c in range(2)]
    across_up = [(i, slabs + i + 1) for i in range(slabs - 1)]
    across_down = [(i + 1, slabs + i) for i in range(slabs - 1)]

    def exchange(x):
        return lax.all_to_all(
            x, "gz", split_axis=0, concat_axis=0, axis_index_groups=groups, tiled=True
        )

    def arrive(levels):
        lev0, lev1, fr, fr0, fr1 = levels
        fr = lax.ppermute(fr, "sec", [(0, 1)])
        fr_lo = lax.ppermute(fr1, ("sec", "gz"), across_up)
        fr_hi = lax.ppermute(fr0, ("sec", "gz"), across_down)
        halo_lo = lax.ppermute(lev1, "gz", up)
        halo_hi = lax.ppermute(lev0, "gz", down)
        return lev0, lev1, fr, halo_lo, halo_hi, fr_lo, fr_hi

    level_shapes = [
        shape(3, nx, ny),
        shape(3, nx, ny),
        shape(2, 3, fringe, ny),
        shape(3, fringe, ny),
        shape(3, fringe, ny),
    ]
    pivots = call(
        functools.partial(pivot_kernel, nx, ny, chips), [], shape(chips, 8, 128), limit=4
    )

    def segment(levels, old):
        lev0, lev1, fr, halo_lo, halo_hi, fr_lo, fr_hi = arrive(levels)
        part = call(
            advect_kernel,
            [idx, lev0, lev1, fr, turbine_mask, dlx, dly],
            shape(2, 3, nx, ny),
            scratch=[(2, 3, nx, ny)],
            smem=1,
            limit=28,
            flops=6 * plane * (nx + ny),
        )
        ins = [idx, lev0, lev1, fr, halo_lo, halo_hi, fr_lo, fr_hi, part, visc]
        scratch = [(2, 3, nx, ny), (2, 3, nx, ny), (3, nx, ny)]
        if old is not None:
            ins += list(old)
            scratch.append((2, 3, nx, ny))
        state, keep, send = call(
            functools.partial(forward_kernel, old is not None),
            ins + list(fore),
            [shape(2, 3, nx, ny), shape(3, half, ny), shape(3, half, ny)],
            scratch=scratch,
            smem=1,
            limit=50,
            flops=3 * plane * (6 * ny + 5 * nx),
        )
        recv = lax.ppermute(send, "gz", swap)
        x = call(
            functools.partial(reduce_kernel, nx, ny, chips),
            [keep, recv],
            shape(chips, 2, 8, 128),
            limit=8,
        )
        x = exchange(x)
        x = call(
            functools.partial(column_kernel, nx, ny, chips),
            [pivots, x],
            shape(chips, 2, 8, 128),
            scratch=[(chips, 8, 128)],
            limit=8,
        )
        x = exchange(x)
        own, send = call(
            functools.partial(expand_kernel, nx, ny, chips),
            [keep, recv, x],
            [shape(3, half, ny), shape(3, half, ny)],
            limit=10,
        )
        recv = lax.ppermute(send, "gz", swap)
        ins = [own, recv, state] + list(back)
        final = old is not None
        outs = call(
            functools.partial(backward_kernel, final),
            ins if final else [idx] + ins,
            shape(3, 2, nx, ny) if final else level_shapes,
            scratch=[(3, nx, ny)],
            smem=0 if final else 1,
            limit=36,
            flops=3 * plane * (6 * ny + 6 * nx),
        )
        return outs, (lev0, lev1, fr)

    levels = call(pack_kernel, [idx, velocity], level_shapes, smem=1, limit=16)
    middle, old = segment(levels, None)
    result, _ = segment(middle, old)
    return result[None]


def solution(mesh):
    placed = (
        P("sec", None, "gz", None, None),
        P("sec", "gz", None, None),
        P("gz", None, None),
        P(),
    )
    return jax.shard_map(
        local,
        mesh=mesh,
        in_specs=placed,
        out_specs=P("sec", None, "gz", None, None),
        check_vma=False,
    )
```

```python
import functools
import math

import jax
import jax.numpy as jnp
import numpy as np
from jax import lax
from jax.experimental import pallas as pl
from jax.experimental.pallas import tpu as pltpu
from jax.sharding import PartitionSpec as P

step_size = 0.1
drag_coef = 0.75
cell_width = 4.0
f32 = jnp.float32
bf16 = jnp.bfloat16
MIB = 1024 * 1024


def derivative_np(n, cutoff):
    i = np.arange(n)
    k = np.arange(1, cutoff + 1)
    wave = 2.0 * np.pi * k / n
    shift = np.sin(2.0 * np.pi / n * ((i[:, None] * k[None, :]) % n)) @ wave
    shift = -(2.0 / (cell_width * n)) * shift
    return shift[(i[:, None] - i[None, :]) % n]


def basis_np(n):
    mid = n // 2
    r = np.arange(n)
    k = np.where(r <= mid, r, r - mid)
    angle = 2.0 * np.pi / n * ((k[:, None] * r[None, :]) % n)
    scale = np.where((r == 0) | (r == mid), math.sqrt(1.0 / n), math.sqrt(2.0 / n))
    return scale[:, None] * np.where((r <= mid)[:, None], np.cos(angle), np.sin(angle))


def basis_slope_np(n):
    slope = basis_np(n) @ derivative_np(n, n // 2 - 1)
    slope[0] = 0.0
    slope[n // 2] = 0.0
    return slope


def hi_lo(table):
    table = np.asarray(table, np.float32)
    hi = table.astype(bf16)
    lo = (table - hi.astype(np.float32)).astype(bf16)
    return np.stack([hi, lo])


def dot(a, b):
    return jnp.dot(a, b, preferred_element_type=f32)


def split(x):
    hi = x.astype(bf16)
    return hi, (x - hi.astype(f32)).astype(bf16)


def left3(t_ref, x):
    hi, lo = split(x)
    return dot(t_ref[0], hi) + (dot(t_ref[1], hi) + dot(t_ref[0], lo))


def right3(x, t_ref):
    hi, lo = split(x)
    return dot(hi, t_ref[0]) + (dot(hi, t_ref[1]) + dot(lo, t_ref[0]))


def wave_gap(row, length):
    mid = length // 2
    k = jnp.where(row < mid, row, jnp.where(row == mid, 0, row - mid)).astype(f32)
    scaled = (2.0 * math.pi / (length * cell_width)) * k
    return scaled * scaled


def tile_gap(first_a, first_b, rows, lanes, nx, ny):
    a = first_a + lax.broadcasted_iota(jnp.int32, (rows, lanes), 0)
    b = first_b + lax.broadcasted_iota(jnp.int32, (rows, lanes), 1)
    return wave_gap(a, nx) + wave_gap(b, ny)


def interior_inverse(mu, is_last):
    det = mu * (mu * mu - 2.0)
    lid = mu * mu * (mu - 1.0) - 2.0 * mu + 1.0
    recip = 1.0 / jnp.where(is_last, lid, det)
    m1 = mu - 1.0
    q11 = jnp.where(is_last, mu * m1 - 1.0, mu * mu - 1.0) * recip
    q12 = jnp.where(is_last, m1, mu) * recip
    q13 = recip
    q22 = jnp.where(is_last, mu * m1, mu * mu) * recip
    q23 = mu * recip
    q33 = (mu * mu - 1.0) * recip
    return q11, q12, q13, q22, q23, q33


def pack_kernel(idx_ref, v_ref, lev0, lev1, fr, fr0, fr1):
    for c in range(3):
        lev0[c] = v_ref[c, 0]
        lev1[c] = v_ref[c, 1]
    pack_rows(idx_ref, (lev0, lev1), fr, fr0, fr1)


def pack_rows(idx_ref, levels, fr, fr0, fr1):
    def body(f, carry):
        row = idx_ref[f]
        for c in range(3):
            low = levels[0][c, pl.ds(row, 1), :]
            high = levels[1][c, pl.ds(row, 1), :]
            fr[0, c, pl.ds(f, 1), :] = low
            fr[1, c, pl.ds(f, 1), :] = high
            fr0[c, pl.ds(f, 1), :] = low
            fr1[c, pl.ds(f, 1), :] = high
        return carry

    lax.fori_loop(0, idx_ref.shape[0], body, 0)


def put_rows(idx_ref, target, source):
    def body(f, carry):
        row = idx_ref[f]
        for c in range(3):
            target[c, pl.ds(row, 1), :] = source[c, pl.ds(f, 1), :]
        return carry

    lax.fori_loop(0, idx_ref.shape[0], body, 0)


def advect_kernel(idx_ref, lev0, lev1, fr, mask, dlx, dly, part, state):
    is_farm = lax.axis_index("sec") == 1
    state[0] = lev0[...]
    state[1] = lev1[...]

    @pl.when(is_farm)
    def _():
        put_rows(idx_ref, state.at[0], fr.at[0])
        put_rows(idx_ref, state.at[1], fr.at[1])

    coef = jnp.where(is_farm, drag_coef, 0.0).astype(f32)
    for z in range(2):
        u = state[z, 0]
        v = state[z, 1]
        drag = coef * mask[z].astype(f32) * jnp.abs(u)
        for c in range(3):
            here = state[z, c]
            r = here.astype(bf16)
            gx = dot(dlx[...], r)
            gy = dot(r, dly[...])
            part[z, c] = -(u * gx + v * gy) - drag * here


def forward_kernel(second, *refs):
    refs = list(refs)
    idx_ref, lev0, lev1, fr, halo_lo, halo_hi, fr_lo, fr_hi, part, visc = refs[:10]
    refs = refs[10:]
    if second:
        old0, old1, old_fr = refs[:3]
        refs = refs[3:]
    by, byd, bx, bxd, vout, keep, send, state, halo, spec = refs[:10]
    if second:
        old = refs[10]
    nx = lev0.shape[1]
    is_farm = lax.axis_index("sec") == 1
    me = lax.axis_index("gz")
    core = lax.rem(me, 2)
    not_lid = (me != lax.axis_size("gz") - 1).astype(f32)
    state[0] = lev0[...]
    state[1] = lev1[...]
    halo[0] = halo_lo[...]
    halo[1] = halo_hi[...]
    if second:
        old[0] = old0[...]
        old[1] = old1[...]

    @pl.when(is_farm)
    def _():
        put_rows(idx_ref, state.at[0], fr.at[0])
        put_rows(idx_ref, state.at[1], fr.at[1])
        put_rows(idx_ref, halo.at[0], fr_lo)
        put_rows(idx_ref, halo.at[1], fr_hi)
        if second:
            put_rows(idx_ref, old.at[0], old_fr.at[0])
            put_rows(idx_ref, old.at[1], old_fr.at[1])

    for z in range(2):
        for c in range(3):
            here = state[z, c]
            below = halo[0, c] if z == 0 else state[0, c]
            above = state[1, c] if z == 0 else halo[1, c]
            tend = part[z, c] - state[z, 2] * (0.5 * (above - below))
            tend = tend + visc[z] * (above - 2.0 * here + below)
            if second:
                new = 0.5 * (old[z, c] + here + step_size * tend)
            else:
                new = here + step_size * tend
            if z == 1 and c == 2:
                new = new * not_lid
            vout[z, c] = new
    w0 = right3(vout[0, 2], by)
    w1 = right3(vout[1, 2], by)
    g0 = right3(vout[0, 1], byd) + w0
    g1 = right3(vout[1, 1], byd) + (w1 - w0)
    spec[0] = left3(bxd, right3(vout[0, 0], by)) + left3(bx, g0)
    spec[1] = left3(bxd, right3(vout[1, 0], by)) + left3(bx, g1)
    spec[2] = left3(bx, w1)
    half = nx // 2
    keep[...] = spec[:, pl.ds(pl.multiple_of(core * half, half), half), :]
    send[...] = spec[:, pl.ds(pl.multiple_of((1 - core) * half, half), half), :]


def sources(core, keep, recv, rows):
    first = core == 0

    def pick(field, low):
        own, other = keep[field, rows, :], recv[field, rows, :]
        return jnp.where(first == low, own, other)

    s1 = pick(1, True)
    s2 = pick(0, False) - pick(2, True)
    s3 = pick(1, False)
    return pick, s1, s2, s3


def own_gap(nx, ny):
    me = lax.axis_index("gz")
    core = lax.rem(me, 2)
    chip = lax.div(me, 2)
    lane_blocks = ny // 128
    first_a = core * (nx // 2) + lax.div(chip, lane_blocks) * 8
    first_b = lax.rem(chip, lane_blocks) * 128
    return tile_gap(first_a, first_b, 8, 128, nx, ny)


def pivot_kernel(nx, ny, chips, pivots):
    eps = own_gap(nx, ny)
    mu = 2.0 + eps
    mm = mu * mu
    inner = mm * eps * (4.0 + eps)
    lid = mm * (mu - 1.0) - 2.0 * mu + 1.0
    last = mu * eps * (mm * mm * (mu + 1.0) - mm * (4.0 * mu + 3.0) + 3.0 * mu + 1.0) / lid
    e = mu * eps * (mm + mu - 1.0)
    pivot = 1.0 / (1.0 + e)
    pivots[0] = pivot

    def body(j, carry):
        e, pivot = carry
        e = inner + e * pivot
        pivot = 1.0 / (1.0 + e)
        pivots[j] = pivot
        return e, pivot

    e, pivot = lax.fori_loop(1, chips - 1, body, (e, pivot))
    e = last + e * pivot
    pivots[chips - 1] = jnp.where(e > 0.0, 1.0 / jnp.where(e > 0.0, e, 1.0), 0.0)


def solve_kernel(
    nx, ny, chips, keep, sent, pivots, own, other, recv, fore, fore_in, back, back_in, work, out, ss, rs
):
    me = lax.axis_index("gz")
    core = lax.rem(me, 2)
    chip = lax.div(me, 2)
    is_last = chip == chips - 1
    half = keep.shape[1]
    lane_blocks = ny // 128
    row_blocks = half // 8
    pieces = 4
    mesh_id = pl.DeviceIdType.MESH
    sibling = {"gz": chip * 2 + (1 - core)}

    def peer(d):
        return {"gz": d * 2 + core}

    def remote(src, dst, lane, to):
        return pltpu.make_async_remote_copy(
            src_ref=src,
            dst_ref=dst,
            send_sem=ss.at[lane],
            recv_sem=rs.at[lane],
            device_id=to,
            device_id_type=mesh_id,
        )

    barrier = pltpu.get_barrier_semaphore()
    pl.semaphore_signal(barrier, inc=1, device_id=sibling, device_id_type=mesh_id)

    def greet(s, carry):
        to = peer(lax.rem(chip + s, chips))
        pl.semaphore_signal(barrier, inc=1, device_id=to, device_id_type=mesh_id)
        return carry

    lax.fori_loop(1, chips, greet, 0)
    pl.semaphore_wait(barrier, chips)

    swap = remote(sent, recv, 0, sibling)
    swap.start()
    swap.wait()

    def reduce(s, carry):
        rb = lax.rem(lax.div(chip, lane_blocks) + s, row_blocks)
        rows = pl.ds(pl.multiple_of(rb * 8, 8), 8)
        pick, s1, s2, s3 = sources(core, keep, recv, rows)
        mu = 2.0 + tile_gap(core * half + rb * 8, 0, 8, ny, nx, ny)
        q11, q12, q13, q22, q23, q33 = interior_inverse(mu, is_last)
        a = -pick(0, True) - (q11 * s1 + q12 * s2 + q13 * s3)
        c = pick(2, False) - (q13 * s1 + q23 * s2 + q33 * s3)
        for lb in range(lane_blocks):
            fore[rb * lane_blocks + lb, 0] = a[:, lb * 128 : (lb + 1) * 128]
            fore[rb * lane_blocks + lb, 1] = c[:, lb * 128 : (lb + 1) * 128]
        return carry

    lax.fori_loop(0, row_blocks, reduce, 0)

    def scatter(source, target, lane):
        def send(s, carry):
            d = lax.rem(chip + s, chips)
            remote(source.at[d], target.at[chip], lane, peer(d)).start()
            return carry

        lax.fori_loop(1, chips, send, 0)
        target[chip] = source[chip]
        most = pl.ds(0, chips - 1)
        everything = remote(source.at[most], target.at[most], lane, sibling)
        everything.wait_recv()
        return everything

    fore_sent = scatter(fore, fore_in, 1)

    mu = 2.0 + own_gap(nx, ny)
    det = mu * (mu * mu - 2.0)
    y = det * fore_in[0, 0] * pivots[0]
    work[0] = y
    for j in range(1, chips):
        y = (det * (fore_in[j, 0] + fore_in[j - 1, 1]) + y) * pivots[j]
        work[j] = y
    back[chips - 1, 0] = y
    back[chips - 1, 1] = jnp.zeros_like(y)
    for j in range(chips - 2, -1, -1):
        back[j, 1] = y
        y = work[j] + y * pivots[j]
        back[j, 0] = y

    back_sent = scatter(back, back_in, 2)

    def expand(rb, carry):
        rows = pl.ds(pl.multiple_of(rb * 8, 8), 8)
        _, s1, s2, s3 = sources(core, keep, recv, rows)
        mu = 2.0 + tile_gap(core * half + rb * 8, 0, 8, ny, nx, ny)
        q11, q12, q13, q22, q23, q33 = interior_inverse(mu, is_last)
        cols = range(lane_blocks)
        p0 = jnp.concatenate([back_in[rb * lane_blocks + lb, 0] for lb in cols], axis=1)
        p4 = jnp.concatenate([back_in[rb * lane_blocks + lb, 1] for lb in cols], axis=1)
        s1 = s1 - p0
        s3 = s3 - p4
        p1 = -(q11 * s1 + q12 * s2 + q13 * s3)
        p2 = -(q12 * s1 + q22 * s2 + q23 * s3)
        p3 = -(q13 * s1 + q23 * s2 + q33 * s3)
        p4 = jnp.where(is_last, p3, p4)
        first = core == 0
        for field, (low, high) in enumerate(((p0, p2), (p1, p3), (p2, p4))):
            own[field, rows, :] = jnp.where(first, low, high)
            out[field, rows, :] = jnp.where(first, high, low)
        return carry

    step = row_blocks // pieces
    for piece in range(pieces):
        lax.fori_loop(piece * step, (piece + 1) * step, expand, 0)
        rows = pl.ds(piece * step * 8, step * 8)
        remote(out.at[:, rows, :], other.at[:, rows, :], 3, sibling).start()
    remote(out, other, 3, sibling).wait()
    fore_sent.wait_send()
    back_sent.wait_send()


def backward_kernel(final, *refs):
    refs = list(refs)
    if not final:
        idx_ref = refs.pop(0)
    own, recv, vin, by, byd, bx, bxd = refs[:7]
    outs = refs[7:-1]
    press = refs[-1]
    half = own.shape[1]
    core = lax.rem(lax.axis_index("gz"), 2)
    press[:, pl.ds(pl.multiple_of(core * half, half), half), :] = own[...]
    press[:, pl.ds(pl.multiple_of((1 - core) * half, half), half), :] = recv[...]
    for z in range(2):
        p = press[z]
        lift = press[z + 1] - p
        new_u = vin[z, 0] - right3(left3(bxd, p), by)
        new_v = vin[z, 1] - right3(left3(bx, p), byd)
        new_w = vin[z, 2] - right3(left3(bx, lift), by)
        for c, new in enumerate((new_u, new_v, new_w)):
            if final:
                outs[0][c, z] = new
            else:
                outs[z][c] = new
    if not final:
        pack_rows(idx_ref, outs[:2], *outs[2:])


VM = pl.BlockSpec(memory_space=pltpu.VMEM)
SM = pl.BlockSpec(memory_space=pltpu.SMEM)


def shape(*dims):
    return jax.ShapeDtypeStruct(dims, f32)


def call(kernel, ins, outs, scratch=(), smem=0, limit=40, flops=0, collective=None):
    many = isinstance(outs, (list, tuple))
    moved = sum(x.size * x.dtype.itemsize for x in ins)
    moved += sum(math.prod(o.shape) * 4 for o in (outs if many else [outs]))
    return pl.pallas_call(
        kernel,
        out_shape=outs,
        in_specs=[SM] * smem + [VM] * (len(ins) - smem),
        out_specs=[VM] * len(outs) if many else VM,
        scratch_shapes=[pltpu.VMEM(s, f32) if isinstance(s, tuple) else s for s in scratch],
        compiler_params=pltpu.CompilerParams(
            vmem_limit_bytes=limit * MIB,
            collective_id=collective,
            has_side_effects=collective is not None,
        ),
        cost_estimate=pl.CostEstimate(flops=flops, bytes_accessed=moved, transcendentals=0),
    )(*ins)


def local(velocity, eddy_viscosity, turbine_mask, idx):
    velocity = velocity[0]
    visc = eddy_viscosity[0]
    _, _, nx, ny = velocity.shape
    fringe = idx.shape[0]
    slabs = lax.axis_size("gz")
    chips = slabs // 2
    half = nx // 2
    plane = 2 * nx * ny

    slope_x, slope_y = basis_slope_np(nx), basis_slope_np(ny)
    base_x, base_y = basis_np(nx), basis_np(ny)
    dlx = jnp.asarray(derivative_np(nx, (nx - 1) // 3).astype(np.float32).astype(bf16))
    dly = jnp.asarray(derivative_np(ny, (ny - 1) // 3).T.astype(np.float32).astype(bf16))
    fore = tuple(jnp.asarray(hi_lo(t)) for t in (base_y.T, slope_y.T, base_x, slope_x))
    back = tuple(jnp.asarray(hi_lo(t)) for t in (base_y, -slope_y, base_x.T, -slope_x.T))

    up = [(i, i + 1) for i in range(slabs - 1)]
    down = [(i + 1, i) for i in range(slabs - 1)]
    across_up = [(i, slabs + i + 1) for i in range(slabs - 1)]
    across_down = [(i + 1, slabs + i) for i in range(slabs - 1)]

    def arrive(levels):
        lev0, lev1, fr, fr0, fr1 = levels
        fr = lax.ppermute(fr, "sec", [(0, 1)])
        fr_lo = lax.ppermute(fr1, ("sec", "gz"), across_up)
        fr_hi = lax.ppermute(fr0, ("sec", "gz"), across_down)
        halo_lo = lax.ppermute(lev1, "gz", up)
        halo_hi = lax.ppermute(lev0, "gz", down)
        return lev0, lev1, fr, halo_lo, halo_hi, fr_lo, fr_hi

    level_shapes = [
        shape(3, nx, ny),
        shape(3, nx, ny),
        shape(2, 3, fringe, ny),
        shape(3, fringe, ny),
        shape(3, fringe, ny),
    ]
    pivots = call(
        functools.partial(pivot_kernel, nx, ny, chips), [], shape(chips, 8, 128), limit=4
    )

    def segment(levels, old):
        lev0, lev1, fr, halo_lo, halo_hi, fr_lo, fr_hi = arrive(levels)
        part = call(
            advect_kernel,
            [idx, lev0, lev1, fr, turbine_mask, dlx, dly],
            shape(2, 3, nx, ny),
            scratch=[(2, 3, nx, ny)],
            smem=1,
            limit=16,
            flops=6 * plane * (nx + ny),
        )
        ins = [idx, lev0, lev1, fr, halo_lo, halo_hi, fr_lo, fr_hi, part, visc]
        scratch = [(2, 3, nx, ny), (2, 3, nx, ny), (3, nx, ny)]
        if old is not None:
            ins += list(old)
            scratch.append((2, 3, nx, ny))
        state, keep, send = call(
            functools.partial(forward_kernel, old is not None),
            ins + list(fore),
            [shape(2, 3, nx, ny), shape(3, half, ny), shape(3, half, ny)],
            scratch=scratch,
            smem=1,
            limit=24,
            flops=3 * plane * (6 * ny + 5 * nx),
        )
        column = (chips, 2, 8, 128)
        own, recv = call(
            functools.partial(solve_kernel, nx, ny, chips),
            [keep, send, pivots],
            [shape(3, half, ny), shape(3, half, ny)],
            scratch=[(3, half, ny)]
            + [column] * 4
            + [(chips, 8, 128), (3, half, ny)]
            + [pltpu.SemaphoreType.DMA((4,))] * 2,
            limit=12,
            collective=0,
        )
        ins = [own, recv, state] + list(back)
        final = old is not None
        outs = call(
            functools.partial(backward_kernel, final),
            ins if final else [idx] + ins,
            shape(3, 2, nx, ny) if final else level_shapes,
            scratch=[(3, nx, ny)],
            smem=0 if final else 1,
            limit=24,
            flops=3 * plane * (6 * ny + 6 * nx),
        )
        return outs, (lev0, lev1, fr)

    levels = call(pack_kernel, [idx, velocity], level_shapes, smem=1, limit=16)
    middle, old = segment(levels, None)
    result, _ = segment(middle, old)
    return result[None]


def solution(mesh):
    placed = (
        P("sec", None, "gz", None, None),
        P("sec", "gz", None, None),
        P("gz", None, None),
        P(),
    )
    return jax.shard_map(
        local,
        mesh=mesh,
        in_specs=placed,
        out_specs=P("sec", None, "gz", None, None),
        check_vma=False,
    )
```

```python
import functools
import math

import jax
import jax.numpy as jnp
import numpy as np
from jax import lax
from jax.experimental import pallas as pl
from jax.experimental.pallas import tpu as pltpu
from jax.sharding import PartitionSpec as P

step_size = 0.1
drag_coef = 0.75
cell_width = 4.0
f32 = jnp.float32
bf16 = jnp.bfloat16
MIB = 1024 * 1024


def derivative_np(n, cutoff):
    i = np.arange(n)
    k = np.arange(1, cutoff + 1)
    wave = 2.0 * np.pi * k / n
    shift = np.sin(2.0 * np.pi / n * ((i[:, None] * k[None, :]) % n)) @ wave
    shift = -(2.0 / (cell_width * n)) * shift
    return shift[(i[:, None] - i[None, :]) % n]


def basis_np(n):
    mid = n // 2
    r = np.arange(n)
    k = np.where(r <= mid, r, r - mid)
    angle = 2.0 * np.pi / n * ((k[:, None] * r[None, :]) % n)
    scale = np.where((r == 0) | (r == mid), math.sqrt(1.0 / n), math.sqrt(2.0 / n))
    return scale[:, None] * np.where((r <= mid)[:, None], np.cos(angle), np.sin(angle))


def basis_slope_np(n):
    slope = basis_np(n) @ derivative_np(n, n // 2 - 1)
    slope[0] = 0.0
    slope[n // 2] = 0.0
    return slope


def hi_lo(table):
    table = np.asarray(table, np.float32)
    hi = table.astype(bf16)
    lo = (table - hi.astype(np.float32)).astype(bf16)
    return np.stack([hi, lo])


def dot(a, b):
    return jnp.dot(a, b, preferred_element_type=f32)


def split(x):
    hi = x.astype(bf16)
    return hi, (x - hi.astype(f32)).astype(bf16)


def left3(t_ref, x):
    hi, lo = split(x)
    return dot(t_ref[0], hi) + (dot(t_ref[1], hi) + dot(t_ref[0], lo))


def right3(x, t_ref):
    hi, lo = split(x)
    return dot(hi, t_ref[0]) + (dot(hi, t_ref[1]) + dot(lo, t_ref[0]))


def wave_gap(row, length):
    mid = length // 2
    k = jnp.where(row < mid, row, jnp.where(row == mid, 0, row - mid)).astype(f32)
    scaled = (2.0 * math.pi / (length * cell_width)) * k
    return scaled * scaled


def tile_gap(first_a, first_b, rows, lanes, nx, ny):
    a = first_a + lax.broadcasted_iota(jnp.int32, (rows, lanes), 0)
    b = first_b + lax.broadcasted_iota(jnp.int32, (rows, lanes), 1)
    return wave_gap(a, nx) + wave_gap(b, ny)


def interior_inverse(mu, is_last):
    det = mu * (mu * mu - 2.0)
    lid = mu * mu * (mu - 1.0) - 2.0 * mu + 1.0
    recip = 1.0 / jnp.where(is_last, lid, det)
    m1 = mu - 1.0
    q11 = jnp.where(is_last, mu * m1 - 1.0, mu * mu - 1.0) * recip
    q12 = jnp.where(is_last, m1, mu) * recip
    q13 = recip
    q22 = jnp.where(is_last, mu * m1, mu * mu) * recip
    q23 = mu * recip
    q33 = (mu * mu - 1.0) * recip
    return q11, q12, q13, q22, q23, q33


def thirds(x):
    high = x.astype(bf16)
    rest = x - high.astype(f32)
    middle = rest.astype(bf16)
    return high, middle, (rest - middle.astype(f32)).astype(bf16)


def remote(src, dst, send_sem, recv_sem, to):
    return pltpu.make_async_remote_copy(
        src_ref=src,
        dst_ref=dst,
        send_sem=send_sem,
        recv_sem=recv_sem,
        device_id=to,
        device_id_type=pl.DeviceIdType.MESH,
    )


def stage_kernel(second, *refs):
    refs = list(refs)
    if second:
        own, other, vin, old, by_b, byd_b, bx_b, bxd_b = refs[:8]
        refs = refs[8:]
    else:
        raw = refs.pop(0)
    wide, tall, mask, visc, dlx, dly, by, byd, bx, bxd = refs[:10]
    vout, keep, send = refs[10:13]
    refs = refs[13:]
    if second:
        now, raw, press = refs[:3]
        refs = refs[3:]
    else:
        now = refs.pop(0)
    part, halo, spec, work, frp, fr, side, pick, covered, hs, hr, fs, fr_sem = refs
    _, _, nx, ny = now.shape
    fringe = fr.shape[2]
    sec = lax.axis_index("sec")
    me = lax.axis_index("gz")
    slabs = lax.axis_size("gz")
    is_farm = sec == 1
    core = lax.rem(me, 2)
    half = nx // 2
    above_id = lax.rem(me + 1, slabs)
    below_id = lax.rem(me + slabs - 1, slabs)
    has_below = (me > 0).astype(f32)
    has_above = (me < slabs - 1).astype(f32)

    barrier = pltpu.get_barrier_semaphore()
    for to in (
        {"sec": sec, "gz": below_id},
        {"sec": sec, "gz": above_id},
        {"sec": 1 - sec, "gz": below_id},
        {"sec": 1 - sec, "gz": me},
        {"sec": 1 - sec, "gz": above_id},
    ):
        pl.semaphore_signal(
            barrier, inc=1, device_id=to, device_id_type=pl.DeviceIdType.MESH
        )
    pl.semaphore_wait(barrier, 5)

    def face(z, c):
        to = {"sec": sec, "gz": lax.rem(me + 2 * z - 1 + slabs, slabs)}
        return remote(raw.at[c, z], halo.at[1 - z, c], hs.at[z, c], hr.at[1 - z, c], to)

    def columns(level):
        farm = 1 - sec
        if level is None:
            return remote(frp, fr, fs.at[2], fr_sem.at[2], {"sec": farm, "gz": me})
        to = {"sec": farm, "gz": (below_id, above_id)[level]}
        return remote(frp.at[level], side.at[1 - level], fs.at[level], fr_sem.at[1 - level], to)

    def project(c, z):
        p = press[z]
        if c == 0:
            raw[c, z] = vin[c, z] - right3(left3(bxd_b, p), by_b)
        elif c == 1:
            raw[c, z] = vin[c, z] - right3(left3(bx_b, p), byd_b)
        else:
            raw[c, z] = vin[c, z] - right3(left3(bx_b, press[z + 1] - p), by_b)

    out_level, in_level = core, 1 - core
    order = (1, 2, 0)
    if second:
        press[:, pl.ds(pl.multiple_of(core * half, half), half), :] = own[...]
        press[:, pl.ds(pl.multiple_of((1 - core) * half, half), half), :] = other[...]
        project(order[0], out_level)
    face(out_level, order[0]).start()
    if second:
        project(order[1], out_level)
        project(order[2], out_level)

        @pl.when(is_farm)
        def _():
            face(out_level, order[1]).start()
            face(out_level, order[2]).start()

        for c in order:
            project(c, in_level)
            face(in_level, c).start()

    @pl.when(jnp.logical_not(is_farm))
    def _():
        hit = lax.broadcasted_iota(jnp.int32, (fringe, nx), 1) == tall[...]
        hit = hit.astype(f32).astype(bf16)
        for z in range(2):
            for c in range(3):
                high, middle, low = thirds(raw[c, z])
                frp[z, c] = (dot(hit, high) + dot(hit, middle)) + dot(hit, low)
        for level in (None, 0, 1):
            columns(level).start()
        if second:
            face(out_level, order[1]).start()
            face(out_level, order[2]).start()

    if not second:
        for c in order[1:]:
            face(out_level, c).start()
        for c in order:
            face(in_level, c).start()

    def placed(rows, here):
        high, middle, low = thirds(rows)
        stack = jnp.concatenate([high, middle, low, jnp.zeros_like(low)], axis=0)
        return jnp.where(covered[...] > 0.5, dot(pick[...], stack), here)

    @pl.when(is_farm)
    def _():
        hit = lax.broadcasted_iota(jnp.int32, (nx, 4 * fringe), 0) == wide[...]
        pick[...] = hit.astype(f32).astype(bf16)
        ones = jnp.ones((fringe, ny), f32)
        ones = jnp.concatenate([ones, jnp.zeros((3 * fringe, ny), f32)], axis=0)
        covered[...] = dot(pick[...], ones.astype(bf16))
        columns(None).wait_recv()
        for z in range(2):
            for c in range(3):
                now[c, z] = placed(fr[z, c], raw[c, z])

    @pl.when(jnp.logical_not(is_farm))
    def _():
        now[...] = raw[...]

    coef = jnp.where(is_farm, drag_coef, 0.0).astype(f32)
    for z in range(2):
        u = now[0, z]
        v = now[1, z]
        drag = coef * mask[z].astype(f32) * jnp.abs(u)
        for c in range(3):
            here = now[c, z]
            r = here.astype(bf16)
            part[c, z] = -(u * dot(dlx[...], r) + v * dot(r, dly[...])) - drag * here

    @pl.when(is_farm)
    def _():
        columns(0).wait_recv()
        columns(1).wait_recv()

    for c in order:
        face(0, c).wait_recv()
        face(1, c).wait_recv()

        @pl.when(is_farm)
        def _():
            for h in range(2):
                work[h] = placed(side[h, c], halo[h, c])

        @pl.when(jnp.logical_not(is_farm))
        def _():
            for h in range(2):
                work[h] = halo[h, c]

        for z in range(2):
            here = now[c, z]
            below = work[0] * has_below if z == 0 else now[c, 0]
            above = work[1] * has_above if z == 1 else now[c, 1]
            tend = part[c, z] - now[2, z] * (0.5 * (above - below))
            tend = tend + visc[z] * (above - 2.0 * here + below)
            if second:
                new = 0.5 * (old[c, z] + here + step_size * tend)
            else:
                new = here + step_size * tend
            if z == 1 and c == 2:
                new = new * has_above
            vout[c, z] = new
        if c == 1:
            for z in range(2):
                spec[z] = right3(vout[1, z], byd)
        elif c == 2:
            w0 = right3(vout[2, 0], by)
            w1 = right3(vout[2, 1], by)
            spec[0] = left3(bx, spec[0] + w0)
            spec[1] = left3(bx, spec[1] + (w1 - w0))
            spec[2] = left3(bx, w1)
        else:
            for z in range(2):
                spec[z] = spec[z] + left3(bxd, right3(vout[0, z], by))
    keep[...] = spec[:, pl.ds(pl.multiple_of(core * half, half), half), :]
    send[...] = spec[:, pl.ds(pl.multiple_of((1 - core) * half, half), half), :]
    for z in range(2):
        for c in range(3):
            face(z, c).wait_send()

    @pl.when(jnp.logical_not(is_farm))
    def _():
        for level in (None, 0, 1):
            columns(level).wait_send()


def sources(core, keep, recv, rows):
    first = core == 0

    def pick(field, low):
        own, other = keep[field, rows, :], recv[field, rows, :]
        return jnp.where(first == low, own, other)

    s1 = pick(1, True)
    s2 = pick(0, False) - pick(2, True)
    s3 = pick(1, False)
    return pick, s1, s2, s3


def own_gap(nx, ny):
    me = lax.axis_index("gz")
    core = lax.rem(me, 2)
    chip = lax.div(me, 2)
    lane_blocks = ny // 128
    first_a = core * (nx // 2) + lax.div(chip, lane_blocks) * 8
    first_b = lax.rem(chip, lane_blocks) * 128
    return tile_gap(first_a, first_b, 8, 128, nx, ny)


def pivot_kernel(nx, ny, chips, pivots):
    eps = own_gap(nx, ny)
    mu = 2.0 + eps
    mm = mu * mu
    inner = mm * eps * (4.0 + eps)
    lid = mm * (mu - 1.0) - 2.0 * mu + 1.0
    last = mu * eps * (mm * mm * (mu + 1.0) - mm * (4.0 * mu + 3.0) + 3.0 * mu + 1.0) / lid
    e = mu * eps * (mm + mu - 1.0)
    pivot = 1.0 / (1.0 + e)
    pivots[0] = pivot

    def body(j, carry):
        e, pivot = carry
        e = inner + e * pivot
        pivot = 1.0 / (1.0 + e)
        pivots[j] = pivot
        return e, pivot

    e, pivot = lax.fori_loop(1, chips - 1, body, (e, pivot))
    e = last + e * pivot
    pivots[chips - 1] = jnp.where(e > 0.0, 1.0 / jnp.where(e > 0.0, e, 1.0), 0.0)


def solve_kernel(
    nx, ny, chips, keep, sent, pivots, own, other, recv, fore, fore_in, back, back_in, work, out, ss, rs
):
    me = lax.axis_index("gz")
    core = lax.rem(me, 2)
    chip = lax.div(me, 2)
    is_last = chip == chips - 1
    half = keep.shape[1]
    lane_blocks = ny // 128
    row_blocks = half // 8
    pieces = 4
    mesh_id = pl.DeviceIdType.MESH
    sibling = {"gz": chip * 2 + (1 - core)}

    def peer(d):
        return {"gz": d * 2 + core}

    def push(src, dst, lane, to):
        return remote(src, dst, ss.at[lane], rs.at[lane], to)

    barrier = pltpu.get_barrier_semaphore()
    pl.semaphore_signal(barrier, inc=1, device_id=sibling, device_id_type=mesh_id)

    def greet(s, carry):
        to = peer(lax.rem(chip + s, chips))
        pl.semaphore_signal(barrier, inc=1, device_id=to, device_id_type=mesh_id)
        return carry

    lax.fori_loop(1, chips, greet, 0)
    pl.semaphore_wait(barrier, chips)

    swap = push(sent, recv, 0, sibling)
    swap.start()
    swap.wait()

    def reduce(s, carry):
        rb = lax.rem(lax.div(chip, lane_blocks) + s, row_blocks)
        rows = pl.ds(pl.multiple_of(rb * 8, 8), 8)
        pick, s1, s2, s3 = sources(core, keep, recv, rows)
        mu = 2.0 + tile_gap(core * half + rb * 8, 0, 8, ny, nx, ny)
        q11, q12, q13, q22, q23, q33 = interior_inverse(mu, is_last)
        a = -pick(0, True) - (q11 * s1 + q12 * s2 + q13 * s3)
        c = pick(2, False) - (q13 * s1 + q23 * s2 + q33 * s3)
        for lb in range(lane_blocks):
            fore[rb * lane_blocks + lb, 0] = a[:, lb * 128 : (lb + 1) * 128]
            fore[rb * lane_blocks + lb, 1] = c[:, lb * 128 : (lb + 1) * 128]
        return carry

    lax.fori_loop(0, row_blocks, reduce, 0)

    def scatter(source, target, lane):
        def send(s, carry):
            d = lax.rem(chip + s, chips)
            push(source.at[d], target.at[chip], lane, peer(d)).start()
            return carry

        lax.fori_loop(1, chips, send, 0)
        target[chip] = source[chip]
        most = pl.ds(0, chips - 1)
        everything = push(source.at[most], target.at[most], lane, sibling)
        everything.wait_recv()
        return everything

    fore_sent = scatter(fore, fore_in, 1)

    mu = 2.0 + own_gap(nx, ny)
    det = mu * (mu * mu - 2.0)
    y = det * fore_in[0, 0] * pivots[0]
    work[0] = y
    for j in range(1, chips):
        y = (det * (fore_in[j, 0] + fore_in[j - 1, 1]) + y) * pivots[j]
        work[j] = y
    back[chips - 1, 0] = y
    back[chips - 1, 1] = jnp.zeros_like(y)
    for j in range(chips - 2, -1, -1):
        back[j, 1] = y
        y = work[j] + y * pivots[j]
        back[j, 0] = y

    back_sent = scatter(back, back_in, 2)

    def expand(rb, carry):
        rows = pl.ds(pl.multiple_of(rb * 8, 8), 8)
        _, s1, s2, s3 = sources(core, keep, recv, rows)
        mu = 2.0 + tile_gap(core * half + rb * 8, 0, 8, ny, nx, ny)
        q11, q12, q13, q22, q23, q33 = interior_inverse(mu, is_last)
        cols = range(lane_blocks)
        p0 = jnp.concatenate([back_in[rb * lane_blocks + lb, 0] for lb in cols], axis=1)
        p4 = jnp.concatenate([back_in[rb * lane_blocks + lb, 1] for lb in cols], axis=1)
        s1 = s1 - p0
        s3 = s3 - p4
        p1 = -(q11 * s1 + q12 * s2 + q13 * s3)
        p2 = -(q12 * s1 + q22 * s2 + q23 * s3)
        p3 = -(q13 * s1 + q23 * s2 + q33 * s3)
        p4 = jnp.where(is_last, p3, p4)
        first = core == 0
        for field, (low, high) in enumerate(((p0, p2), (p1, p3), (p2, p4))):
            own[field, rows, :] = jnp.where(first, low, high)
            out[field, rows, :] = jnp.where(first, high, low)
        return carry

    step = row_blocks // pieces
    for piece in range(pieces):
        lax.fori_loop(piece * step, (piece + 1) * step, expand, 0)
        rows = pl.ds(piece * step * 8, step * 8)
        push(out.at[:, rows, :], other.at[:, rows, :], 3, sibling).start()
    push(out, other, 3, sibling).wait()
    fore_sent.wait_send()
    back_sent.wait_send()


def backward_kernel(own, other, vin, by, byd, bx, bxd, out, press):
    half = own.shape[1]
    core = lax.rem(lax.axis_index("gz"), 2)
    press[:, pl.ds(pl.multiple_of(core * half, half), half), :] = own[...]
    press[:, pl.ds(pl.multiple_of((1 - core) * half, half), half), :] = other[...]
    for z in range(2):
        p = press[z]
        lift = press[z + 1] - p
        out[0, z] = vin[0, z] - right3(left3(bxd, p), by)
        out[1, z] = vin[1, z] - right3(left3(bx, p), byd)
        out[2, z] = vin[2, z] - right3(left3(bx, lift), by)


VM = pl.BlockSpec(memory_space=pltpu.VMEM)


def shape(*dims):
    return jax.ShapeDtypeStruct(dims, f32)


def call(kernel, ins, outs, scratch=(), limit=40, flops=0, collective=None):
    many = isinstance(outs, (list, tuple))
    moved = sum(x.size * x.dtype.itemsize for x in ins)
    moved += sum(math.prod(o.shape) * 4 for o in (outs if many else [outs]))
    return pl.pallas_call(
        kernel,
        out_shape=outs,
        in_specs=[VM] * len(ins),
        out_specs=[VM] * len(outs) if many else VM,
        scratch_shapes=[pltpu.VMEM(s, f32) if isinstance(s, tuple) else s for s in scratch],
        compiler_params=pltpu.CompilerParams(
            vmem_limit_bytes=limit * MIB,
            collective_id=collective,
            has_side_effects=collective is not None,
        ),
        cost_estimate=pl.CostEstimate(flops=flops, bytes_accessed=moved, transcendentals=0),
    )(*ins)


def local(velocity, eddy_viscosity, turbine_mask, idx):
    velocity = velocity[0]
    visc = eddy_viscosity[0]
    _, _, nx, ny = velocity.shape
    fringe = idx.shape[0]
    slabs = lax.axis_size("gz")
    chips = slabs // 2
    half = nx // 2
    plane = 2 * nx * ny

    slope_x, slope_y = basis_slope_np(nx), basis_slope_np(ny)
    base_x, base_y = basis_np(nx), basis_np(ny)
    dlx = jnp.asarray(derivative_np(nx, (nx - 1) // 3).astype(np.float32).astype(bf16))
    dly = jnp.asarray(derivative_np(ny, (ny - 1) // 3).T.astype(np.float32).astype(bf16))
    fore = tuple(jnp.asarray(hi_lo(t)) for t in (base_y.T, slope_y.T, base_x, slope_x))
    back = tuple(jnp.asarray(hi_lo(t)) for t in (base_y, -slope_y, base_x.T, -slope_x.T))

    wide = jnp.concatenate([idx, idx, idx, jnp.full_like(idx, -1)])[None, :]
    tall = idx[:, None]
    field = (3, 2, nx, ny)
    dma = pltpu.SemaphoreType.DMA
    pivots = call(
        functools.partial(pivot_kernel, nx, ny, chips), [], shape(chips, 8, 128), limit=4
    )
    stage_out = [shape(*field), shape(3, half, ny), shape(3, half, ny)]
    stage_scratch = [
        field,
        (2, 3, nx, ny),
        (3, nx, ny),
        (2, nx, ny),
        (2, 3, fringe, ny),
        (2, 3, fringe, ny),
        (2, 3, fringe, ny),
        pltpu.VMEM((nx, 4 * fringe), bf16),
        (nx, ny),
        dma((2, 3)),
        dma((2, 3)),
        dma((3,)),
        dma((3,)),
    ]
    shared = [wide, tall, turbine_mask, visc, dlx, dly] + list(fore)
    ahead = plane * (6 * nx + 6 * ny) + 3 * plane * (6 * ny + 5 * nx)

    def solve(keep, send):
        column = (chips, 2, 8, 128)
        return call(
            functools.partial(solve_kernel, nx, ny, chips),
            [keep, send, pivots],
            [shape(3, half, ny), shape(3, half, ny)],
            scratch=[(3, half, ny)]
            + [column] * 4
            + [(chips, 8, 128), (3, half, ny)]
            + [dma((4,))] * 2,
            limit=12,
            collective=0,
        )

    state, keep, send, start = call(
        functools.partial(stage_kernel, False),
        [velocity] + shared,
        stage_out + [shape(*field)],
        scratch=stage_scratch,
        limit=22,
        flops=ahead,
        collective=1,
    )
    own, other = solve(keep, send)
    state, keep, send = call(
        functools.partial(stage_kernel, True),
        [own, other, state, start] + list(back) + shared,
        stage_out,
        scratch=[field, field, (3, nx, ny)] + stage_scratch,
        limit=28,
        flops=ahead + 3 * plane * (6 * ny + 6 * nx),
        collective=2,
    )
    own, other = solve(keep, send)
    result = call(
        backward_kernel,
        [own, other, state] + list(back),
        shape(*field),
        scratch=[(3, nx, ny)],
        limit=16,
        flops=3 * plane * (6 * ny + 6 * nx),
    )
    return result[None]


def solution(mesh):
    placed = (
        P("sec", None, "gz", None, None),
        P("sec", "gz", None, None),
        P("gz", None, None),
        P(),
    )
    return jax.shard_map(
        local,
        mesh=mesh,
        in_specs=placed,
        out_specs=P("sec", None, "gz", None, None),
        check_vma=False,
    )
```

```python
import functools
import math

import jax
import jax.numpy as jnp
import numpy as np
from jax import lax
from jax.experimental import pallas as pl
from jax.experimental.pallas import tpu as pltpu
from jax.sharding import PartitionSpec as P

step_size = 0.1
drag_coef = 0.75
cell_width = 4.0
f32 = jnp.float32
bf16 = jnp.bfloat16
MIB = 1024 * 1024


def derivative_np(n, cutoff):
    i = np.arange(n)
    k = np.arange(1, cutoff + 1)
    wave = 2.0 * np.pi * k / n
    shift = np.sin(2.0 * np.pi / n * ((i[:, None] * k[None, :]) % n)) @ wave
    shift = -(2.0 / (cell_width * n)) * shift
    return shift[(i[:, None] - i[None, :]) % n]


def basis_np(n):
    mid = n // 2
    r = np.arange(n)
    k = np.where(r <= mid, r, r - mid)
    angle = 2.0 * np.pi / n * ((k[:, None] * r[None, :]) % n)
    scale = np.where((r == 0) | (r == mid), math.sqrt(1.0 / n), math.sqrt(2.0 / n))
    return scale[:, None] * np.where((r <= mid)[:, None], np.cos(angle), np.sin(angle))


def basis_slope_np(n):
    slope = basis_np(n) @ derivative_np(n, n // 2 - 1)
    slope[0] = 0.0
    slope[n // 2] = 0.0
    return slope


def hi_lo(table):
    table = np.asarray(table, np.float32)
    hi = table.astype(bf16)
    lo = (table - hi.astype(np.float32)).astype(bf16)
    return np.stack([hi, lo])


def by_parity(table):
    mid = table.shape[0] // 2
    even = list(range(0, mid + 1, 2)) + list(range(mid + 2, 2 * mid, 2))
    odd = list(range(1, mid, 2)) + list(range(mid + 1, 2 * mid, 2))
    return np.stack([table[even][:, :mid], table[odd][:, :mid]])


def stacked(halves):
    return np.stack([np.concatenate(list(hi_lo(half))) for half in halves])


def dot(a, b):
    return jnp.dot(a, b, preferred_element_type=f32)


def split(x):
    hi = x.astype(bf16)
    return hi, (x - hi.astype(f32)).astype(bf16)


def half3(t_ref, h, x):
    mid = x.shape[0]
    hi, lo = split(x)
    both = dot(t_ref[h], hi)
    return both[:mid] + (both[mid:] + dot(t_ref[h, :mid, :], lo))


def fore3(t_ref, x):
    mid = x.shape[0] // 2
    low, high = x[:mid], x[mid:]
    even = half3(t_ref, 0, low + high)
    odd = half3(t_ref, 1, low - high)
    return jnp.concatenate([even, odd], axis=0)


def back3(t_ref, x):
    mid = x.shape[0] // 2
    even = half3(t_ref, 0, x[:mid])
    odd = half3(t_ref, 1, x[mid:])
    return jnp.concatenate([even + odd, even - odd], axis=0)


def right3(x, t_ref):
    hi, lo = split(x)
    return dot(hi, t_ref[0]) + (dot(hi, t_ref[1]) + dot(lo, t_ref[0]))


def wave_gap(row, length):
    mid = length // 2
    k = jnp.where(row < mid, row, jnp.where(row == mid, 0, row - mid)).astype(f32)
    scaled = (2.0 * math.pi / (length * cell_width)) * k
    return scaled * scaled


def parity_gap(row, length):
    mid = length // 2
    odd = row >= mid
    place = row - jnp.where(odd, mid, 0)
    place = place - jnp.where(place < mid // 2, 0, mid // 2)
    k = (2 * place + jnp.where(odd, 1, 0)).astype(f32)
    scaled = (2.0 * math.pi / (length * cell_width)) * k
    return scaled * scaled


def tile_gap(first_a, first_b, rows, lanes, nx, ny):
    a = first_a + lax.broadcasted_iota(jnp.int32, (rows, lanes), 0)
    b = first_b + lax.broadcasted_iota(jnp.int32, (rows, lanes), 1)
    return parity_gap(a, nx) + wave_gap(b, ny)


def interior_inverse(mu, is_last):
    det = mu * (mu * mu - 2.0)
    lid = mu * mu * (mu - 1.0) - 2.0 * mu + 1.0
    recip = 1.0 / jnp.where(is_last, lid, det)
    m1 = mu - 1.0
    q11 = jnp.where(is_last, mu * m1 - 1.0, mu * mu - 1.0) * recip
    q12 = jnp.where(is_last, m1, mu) * recip
    q13 = recip
    q22 = jnp.where(is_last, mu * m1, mu * mu) * recip
    q23 = mu * recip
    q33 = (mu * mu - 1.0) * recip
    return q11, q12, q13, q22, q23, q33


def thirds(x):
    high = x.astype(bf16)
    rest = x - high.astype(f32)
    middle = rest.astype(bf16)
    return high, middle, (rest - middle.astype(f32)).astype(bf16)


def remote(src, dst, send_sem, recv_sem, to):
    return pltpu.make_async_remote_copy(
        src_ref=src,
        dst_ref=dst,
        send_sem=send_sem,
        recv_sem=recv_sem,
        device_id=to,
        device_id_type=pl.DeviceIdType.MESH,
    )


def stage_kernel(second, *refs):
    refs = list(refs)
    idx_ref = refs.pop(0)
    if second:
        own, other, vin, old, by_b, byd_b, bx_b, bxd_b = refs[:8]
        refs = refs[8:]
    else:
        raw = refs.pop(0)
    tables = refs[:8]
    vout, keep, recv = refs[8:11]
    refs = refs[11:]
    if second:
        now, sent, press = refs[:3]
        raw = sent
        refs = refs[3:]
    else:
        now, pivots, sent = refs[:3]
        local_tables = refs[3:11]
        load_sem = refs[11]
        refs = refs[12:]
        loads = [pltpu.make_async_copy(raw, sent, load_sem.at[0])]
        for i, (source, target) in enumerate(zip(tables, local_tables)):
            loads.append(pltpu.make_async_copy(source, target, load_sem.at[i + 1]))
        for load in loads:
            load.start()
        tables = local_tables
    mask, visc, dlx, dly, by, byd, bx, bxd = tables
    part, halo, spec, work, frp, fr, side, pick, covered, hs, hr, fs, fr_sem, xs, xr = refs
    _, _, nx, ny = now.shape
    fringe = fr.shape[2]
    sec = lax.axis_index("sec")
    me = lax.axis_index("gz")
    slabs = lax.axis_size("gz")
    is_farm = sec == 1
    core = lax.rem(me, 2)
    half = nx // 2
    above_id = lax.rem(me + 1, slabs)
    below_id = lax.rem(me + slabs - 1, slabs)
    has_below = (me > 0).astype(f32)
    has_above = (me < slabs - 1).astype(f32)

    barrier = pltpu.get_barrier_semaphore()
    for to in (
        {"sec": sec, "gz": below_id},
        {"sec": sec, "gz": above_id},
        {"sec": 1 - sec, "gz": below_id},
        {"sec": 1 - sec, "gz": me},
        {"sec": 1 - sec, "gz": above_id},
    ):
        pl.semaphore_signal(
            barrier, inc=1, device_id=to, device_id_type=pl.DeviceIdType.MESH
        )
    pl.semaphore_wait(barrier, 5)

    def face(z, c):
        to = {"sec": sec, "gz": lax.rem(me + 2 * z - 1 + slabs, slabs)}
        return remote(raw.at[c, z], halo.at[1 - z, c], hs.at[z, c], hr.at[1 - z, c], to)

    def columns(level):
        farm = 1 - sec
        if level is None:
            return remote(frp, fr, fs.at[2], fr_sem.at[2], {"sec": farm, "gz": me})
        to = {"sec": farm, "gz": (below_id, above_id)[level]}
        return remote(frp.at[level], side.at[1 - level], fs.at[level], fr_sem.at[1 - level], to)

    def trade(field):
        rows = pl.ds(pl.multiple_of((1 - core) * half, half), half)
        to = {"sec": sec, "gz": me + 1 - 2 * core}
        return remote(spec.at[field, rows, :], recv.at[field], xs.at[field], xr.at[field], to)

    def project(c, z):
        p = press[z]
        if c == 0:
            raw[c, z] = vin[c, z] - right3(back3(bxd_b, p), by_b)
        elif c == 1:
            raw[c, z] = vin[c, z] - right3(back3(bx_b, p), byd_b)
        else:
            raw[c, z] = vin[c, z] - right3(back3(bx_b, press[z + 1] - p), by_b)

    out_level, in_level = core, 1 - core
    order = (1, 2, 0)
    if second:
        press[:, pl.ds(pl.multiple_of(core * half, half), half), :] = own[...]
        press[:, pl.ds(pl.multiple_of((1 - core) * half, half), half), :] = other[...]
        project(order[0], out_level)
    face(out_level, order[0]).start()
    if second:
        project(order[1], out_level)
        project(order[2], out_level)

        @pl.when(is_farm)
        def _():
            face(out_level, order[1]).start()
            face(out_level, order[2]).start()

        for c in order:
            project(c, in_level)
            face(in_level, c).start()

    if not second:
        loads[0].wait()

    @pl.when(jnp.logical_not(is_farm))
    def _():
        place = lax.broadcasted_iota(jnp.int32, (fringe, 1), 0)
        tall = jnp.full((fringe, 1), -1, jnp.int32)
        for f in range(fringe):
            tall = jnp.where(place == f, idx_ref[f], tall)
        hit = lax.broadcasted_iota(jnp.int32, (fringe, nx), 1) == tall
        hit = hit.astype(f32).astype(bf16)
        for z in range(2):
            for c in range(3):
                high, middle, low = thirds(sent[c, z])
                frp[z, c] = (dot(hit, high) + dot(hit, middle)) + dot(hit, low)
        for level in (None, 0, 1):
            columns(level).start()
        if second:
            face(out_level, order[1]).start()
            face(out_level, order[2]).start()

    if not second:
        for c in order[1:]:
            face(out_level, c).start()
        for c in order:
            face(in_level, c).start()
        pivot_table(nx, ny, slabs // 2, pivots)

    def placed(rows, here):
        high, middle, low = thirds(rows)
        stack = jnp.concatenate([high, middle, low, jnp.zeros_like(low)], axis=0)
        return jnp.where(covered[...] > 0.5, dot(pick[...], stack), here)

    @pl.when(is_farm)
    def _():
        lane = lax.broadcasted_iota(jnp.int32, (1, 4 * fringe), 1)
        wide = jnp.full((1, 4 * fringe), -1, jnp.int32)
        for f in range(fringe):
            here = (lane == f) | (lane == f + fringe) | (lane == f + 2 * fringe)
            wide = jnp.where(here, idx_ref[f], wide)
        hit = lax.broadcasted_iota(jnp.int32, (nx, 4 * fringe), 0) == wide
        pick[...] = hit.astype(f32).astype(bf16)
        ones = jnp.ones((fringe, ny), f32)
        ones = jnp.concatenate([ones, jnp.zeros((3 * fringe, ny), f32)], axis=0)
        covered[...] = dot(pick[...], ones.astype(bf16))
        columns(None).wait_recv()
        for z in range(2):
            for c in range(3):
                now[c, z] = placed(fr[z, c], sent[c, z])

    @pl.when(jnp.logical_not(is_farm))
    def _():
        now[...] = sent[...]

    if not second:
        for load in loads[1:]:
            load.wait()
    coef = jnp.where(is_farm, drag_coef, 0.0).astype(f32)
    for z in range(2):
        u = now[0, z]
        v = now[1, z]
        drag = coef * mask[z].astype(f32) * jnp.abs(u)
        for c in range(3):
            here = now[c, z]
            r = here.astype(bf16)
            part[c, z] = -(u * dot(dlx[...], r) + v * dot(r, dly[...])) - drag * here

    @pl.when(is_farm)
    def _():
        columns(0).wait_recv()
        columns(1).wait_recv()

    for c in order:
        face(0, c).wait_recv()
        face(1, c).wait_recv()

        @pl.when(is_farm)
        def _():
            for h in range(2):
                work[h] = placed(side[h, c], halo[h, c])

        @pl.when(jnp.logical_not(is_farm))
        def _():
            for h in range(2):
                work[h] = halo[h, c]

        for z in range(2):
            here = now[c, z]
            below = work[0] * has_below if z == 0 else now[c, 0]
            above = work[1] * has_above if z == 1 else now[c, 1]
            tend = part[c, z] - now[2, z] * (0.5 * (above - below))
            tend = tend + visc[z] * (above - 2.0 * here + below)
            if second:
                new = 0.5 * (old[c, z] + here + step_size * tend)
            else:
                new = here + step_size * tend
            if z == 1 and c == 2:
                new = new * has_above
            vout[c, z] = new
        if c == 1:
            for z in range(2):
                spec[z] = right3(vout[1, z], byd)
        elif c == 2:
            w0 = right3(vout[2, 0], by)
            w1 = right3(vout[2, 1], by)
            spec[0] = fore3(bx, spec[0] + w0)
            spec[1] = fore3(bx, spec[1] + (w1 - w0))
            spec[2] = fore3(bx, w1)
            trade(2).start()
        else:
            for z in range(2):
                spec[z] = spec[z] + fore3(bxd, right3(vout[0, z], by))
                trade(z).start()
    keep[...] = spec[:, pl.ds(pl.multiple_of(core * half, half), half), :]
    for field in range(3):
        trade(field).wait()
    for z in range(2):
        for c in range(3):
            face(z, c).wait_send()

    @pl.when(jnp.logical_not(is_farm))
    def _():
        for level in (None, 0, 1):
            columns(level).wait_send()


def sources(core, keep, recv, rows):
    first = core == 0

    def pick(field, low):
        own, other = keep[field, rows, :], recv[field, rows, :]
        return jnp.where(first == low, own, other)

    s1 = pick(1, True)
    s2 = pick(0, False) - pick(2, True)
    s3 = pick(1, False)
    return pick, s1, s2, s3


def own_gap(nx, ny):
    me = lax.axis_index("gz")
    core = lax.rem(me, 2)
    chip = lax.div(me, 2)
    lane_blocks = ny // 128
    first_a = core * (nx // 2) + lax.div(chip, lane_blocks) * 8
    first_b = lax.rem(chip, lane_blocks) * 128
    return tile_gap(first_a, first_b, 8, 128, nx, ny)


def pivot_table(nx, ny, chips, pivots):
    eps = own_gap(nx, ny)
    mu = 2.0 + eps
    mm = mu * mu
    inner = mm * eps * (4.0 + eps)
    lid = mm * (mu - 1.0) - 2.0 * mu + 1.0
    last = mu * eps * (mm * mm * (mu + 1.0) - mm * (4.0 * mu + 3.0) + 3.0 * mu + 1.0) / lid
    e = mu * eps * (mm + mu - 1.0)
    pivot = 1.0 / (1.0 + e)
    pivots[0] = pivot

    def body(j, carry):
        e, pivot = carry
        e = inner + e * pivot
        pivot = 1.0 / (1.0 + e)
        pivots[j] = pivot
        return e, pivot

    e, pivot = lax.fori_loop(1, chips - 1, body, (e, pivot))
    e = last + e * pivot
    pivots[chips - 1] = jnp.where(e > 0.0, 1.0 / jnp.where(e > 0.0, e, 1.0), 0.0)


def solve_kernel(
    nx, ny, chips, keep, recv, pivots, own, other, fore, fore_in, back, back_in, work, out, ss, rs
):
    me = lax.axis_index("gz")
    core = lax.rem(me, 2)
    chip = lax.div(me, 2)
    is_last = chip == chips - 1
    half = keep.shape[1]
    lane_blocks = ny // 128
    row_blocks = half // 8
    pieces = 4
    mesh_id = pl.DeviceIdType.MESH
    sibling = {"gz": chip * 2 + (1 - core)}

    def peer(d):
        return {"gz": d * 2 + core}

    def push(src, dst, lane, to):
        return remote(src, dst, ss.at[lane], rs.at[lane], to)

    barrier = pltpu.get_barrier_semaphore()
    pl.semaphore_signal(barrier, inc=1, device_id=sibling, device_id_type=mesh_id)

    def greet(s, carry):
        to = peer(lax.rem(chip + s, chips))
        pl.semaphore_signal(barrier, inc=1, device_id=to, device_id_type=mesh_id)
        return carry

    lax.fori_loop(1, chips, greet, 0)

    def reduce(s, carry):
        rb = lax.rem(lax.div(chip, lane_blocks) + s, row_blocks)
        rows = pl.ds(pl.multiple_of(rb * 8, 8), 8)
        pick, s1, s2, s3 = sources(core, keep, recv, rows)
        mu = 2.0 + tile_gap(core * half + rb * 8, 0, 8, ny, nx, ny)
        q11, q12, q13, q22, q23, q33 = interior_inverse(mu, is_last)
        a = -pick(0, True) - (q11 * s1 + q12 * s2 + q13 * s3)
        c = pick(2, False) - (q13 * s1 + q23 * s2 + q33 * s3)
        for lb in range(lane_blocks):
            fore[rb * lane_blocks + lb, 0] = a[:, lb * 128 : (lb + 1) * 128]
            fore[rb * lane_blocks + lb, 1] = c[:, lb * 128 : (lb + 1) * 128]
        return carry

    lax.fori_loop(0, row_blocks, reduce, 0)
    pl.semaphore_wait(barrier, chips)

    def scatter(source, target, lane):
        def send(s, carry):
            d = lax.rem(chip + s, chips)
            push(source.at[d], target.at[chip], lane, peer(d)).start()
            return carry

        lax.fori_loop(1, chips, send, 0)
        target[chip] = source[chip]
        most = pl.ds(0, chips - 1)
        everything = push(source.at[most], target.at[most], lane, sibling)
        everything.wait_recv()
        return everything

    fore_sent = scatter(fore, fore_in, 1)

    mu = 2.0 + own_gap(nx, ny)
    det = mu * (mu * mu - 2.0)
    y = det * fore_in[0, 0] * pivots[0]
    work[0] = y
    for j in range(1, chips):
        y = (det * (fore_in[j, 0] + fore_in[j - 1, 1]) + y) * pivots[j]
        work[j] = y
    back[chips - 1, 0] = y
    back[chips - 1, 1] = jnp.zeros_like(y)
    for j in range(chips - 2, -1, -1):
        back[j, 1] = y
        y = work[j] + y * pivots[j]
        back[j, 0] = y

    back_sent = scatter(back, back_in, 2)

    def expand(rb, carry):
        rows = pl.ds(pl.multiple_of(rb * 8, 8), 8)
        _, s1, s2, s3 = sources(core, keep, recv, rows)
        mu = 2.0 + tile_gap(core * half + rb * 8, 0, 8, ny, nx, ny)
        q11, q12, q13, q22, q23, q33 = interior_inverse(mu, is_last)
        cols = range(lane_blocks)
        p0 = jnp.concatenate([back_in[rb * lane_blocks + lb, 0] for lb in cols], axis=1)
        p4 = jnp.concatenate([back_in[rb * lane_blocks + lb, 1] for lb in cols], axis=1)
        s1 = s1 - p0
        s3 = s3 - p4
        p1 = -(q11 * s1 + q12 * s2 + q13 * s3)
        p2 = -(q12 * s1 + q22 * s2 + q23 * s3)
        p3 = -(q13 * s1 + q23 * s2 + q33 * s3)
        p4 = jnp.where(is_last, p3, p4)
        first = core == 0
        for field, (low, high) in enumerate(((p0, p2), (p1, p3), (p2, p4))):
            own[field, rows, :] = jnp.where(first, low, high)
            out[field, rows, :] = jnp.where(first, high, low)
        return carry

    step = row_blocks // pieces
    for piece in range(pieces):
        lax.fori_loop(piece * step, (piece + 1) * step, expand, 0)
        rows = pl.ds(piece * step * 8, step * 8)
        push(out.at[:, rows, :], other.at[:, rows, :], 0, sibling).start()
    push(out, other, 0, sibling).wait()
    fore_sent.wait_send()
    back_sent.wait_send()


def backward_kernel(own, other, vin, by, byd, bx, bxd, out, press, new, sems):
    half = own.shape[1]
    core = lax.rem(lax.axis_index("gz"), 2)
    press[:, pl.ds(pl.multiple_of(core * half, half), half), :] = own[...]
    press[:, pl.ds(pl.multiple_of((1 - core) * half, half), half), :] = other[...]
    copies = []

    def finish(c, z, correction):
        new[c, z] = vin[c, z] - correction
        copies.append(pltpu.make_async_copy(new.at[c, z], out.at[c, z], sems.at[c, z]))
        copies[-1].start()

    for z in range(2):
        p = press[z]
        lift = press[z + 1] - p
        finish(0, z, right3(back3(bxd, p), by))
        finish(1, z, right3(back3(bx, p), byd))
        finish(2, z, right3(back3(bx, lift), by))
    for copy in copies:
        copy.wait()


VM = pl.BlockSpec(memory_space=pltpu.VMEM)
SM = pl.BlockSpec(memory_space=pltpu.SMEM)
HB = pl.BlockSpec(memory_space=pltpu.HBM)


def shape(*dims):
    return jax.ShapeDtypeStruct(dims, f32)


def call(kernel, ins, outs, scratch=(), limit=40, flops=0, collective=None, specs=None, to=VM):
    many = isinstance(outs, (list, tuple))
    moved = sum(x.size * x.dtype.itemsize for x in ins)
    moved += sum(math.prod(o.shape) * 4 for o in (outs if many else [outs]))
    return pl.pallas_call(
        kernel,
        out_shape=outs,
        in_specs=specs or [VM] * len(ins),
        out_specs=[to] * len(outs) if many else to,
        scratch_shapes=[pltpu.VMEM(s, f32) if isinstance(s, tuple) else s for s in scratch],
        compiler_params=pltpu.CompilerParams(
            vmem_limit_bytes=limit * MIB,
            collective_id=collective,
            has_side_effects=collective is not None,
        ),
        cost_estimate=pl.CostEstimate(flops=flops, bytes_accessed=moved, transcendentals=0),
    )(*ins)


def local(velocity, eddy_viscosity, turbine_mask, idx):
    velocity = velocity[0]
    visc = eddy_viscosity[0]
    _, _, nx, ny = velocity.shape
    fringe = idx.shape[0]
    slabs = lax.axis_size("gz")
    chips = slabs // 2
    half = nx // 2
    plane = 2 * nx * ny

    slope_x, slope_y = by_parity(basis_slope_np(nx)), basis_slope_np(ny)
    base_x, base_y = by_parity(basis_np(nx)), basis_np(ny)
    turned = (0, 2, 1)
    dlx = jnp.asarray(derivative_np(nx, (nx - 1) // 3).astype(np.float32).astype(bf16))
    dly = jnp.asarray(derivative_np(ny, (ny - 1) // 3).T.astype(np.float32).astype(bf16))
    fore = [hi_lo(base_y.T), hi_lo(slope_y.T), stacked(base_x), stacked(slope_x)]
    back = [
        hi_lo(base_y),
        hi_lo(-slope_y),
        stacked(base_x.transpose(turned)),
        stacked(-slope_x.transpose(turned)),
    ]
    fore = [jnp.asarray(t) for t in fore]
    back = [jnp.asarray(t) for t in back]
    field = (3, 2, nx, ny)
    dma = pltpu.SemaphoreType.DMA
    stage_out = [shape(*field), shape(3, half, ny), shape(3, half, ny)]
    stage_scratch = [
        field,
        (2, 3, nx, ny),
        (3, nx, ny),
        (2, nx, ny),
        (2, 3, fringe, ny),
        (2, 3, fringe, ny),
        (2, 3, fringe, ny),
        pltpu.VMEM((nx, 4 * fringe), bf16),
        (nx, ny),
        dma((2, 3)),
        dma((2, 3)),
        dma((3,)),
        dma((3,)),
        dma((3,)),
        dma((3,)),
    ]
    shared = [turbine_mask, visc, dlx, dly] + fore
    ahead = plane * (6 * nx + 6 * ny) + 3 * plane * (6 * ny + 5 * nx)

    def solve(keep, recv, pivots):
        column = (chips, 2, 8, 128)
        return call(
            functools.partial(solve_kernel, nx, ny, chips),
            [keep, recv, pivots],
            [shape(3, half, ny), shape(3, half, ny)],
            scratch=[column] * 4 + [(chips, 8, 128), (3, half, ny)] + [dma((3,))] * 2,
            limit=12,
            collective=0,
        )

    loaded = [field] + [pltpu.VMEM(t.shape, t.dtype) for t in shared] + [dma((9,))]
    state, keep, recv, start, pivots = call(
        functools.partial(stage_kernel, False),
        [idx] + [pltpu.with_memory_space_constraint(x, pltpu.HBM) for x in [velocity] + shared],
        stage_out + [shape(*field), shape(chips, 8, 128)],
        scratch=loaded + stage_scratch,
        limit=30,
        flops=ahead,
        collective=1,
        specs=[SM] + [HB] * (1 + len(shared)),
    )
    own, other = solve(keep, recv, pivots)
    state, keep, recv = call(
        functools.partial(stage_kernel, True),
        [idx, own, other, state, start] + back + shared,
        stage_out,
        scratch=[field, field, (3, nx, ny)] + stage_scratch,
        limit=28,
        flops=ahead + 3 * plane * (6 * ny + 6 * nx),
        collective=2,
        specs=[SM] + [VM] * (8 + len(shared)),
    )
    own, other = solve(keep, recv, pivots)
    result = call(
        backward_kernel,
        [own, other, state] + back,
        shape(*field),
        scratch=[(3, nx, ny), field, dma((3, 2))],
        limit=16,
        flops=3 * plane * (6 * ny + 6 * nx),
        to=HB,
    )
    return result[None]


def solution(mesh):
    placed = (
        P("sec", None, "gz", None, None),
        P("sec", "gz", None, None),
        P("gz", None, None),
        P(),
    )
    return jax.shard_map(
        local,
        mesh=mesh,
        in_specs=placed,
        out_specs=P("sec", None, "gz", None, None),
        check_vma=False,
    )
```

```python
import functools
import math

import jax
import jax.numpy as jnp
import numpy as np
from jax import lax
from jax.experimental import pallas as pl
from jax.experimental.pallas import tpu as pltpu
from jax.sharding import PartitionSpec as P

step_size = 0.1
drag_coef = 0.75
cell_width = 4.0
f32 = jnp.float32
bf16 = jnp.bfloat16
MIB = 1024 * 1024


def derivative_np(n, cutoff):
    i = np.arange(n)
    k = np.arange(1, cutoff + 1)
    wave = 2.0 * np.pi * k / n
    shift = np.sin(2.0 * np.pi / n * ((i[:, None] * k[None, :]) % n)) @ wave
    shift = -(2.0 / (cell_width * n)) * shift
    return shift[(i[:, None] - i[None, :]) % n]


def basis_np(n):
    mid = n // 2
    r = np.arange(n)
    k = np.where(r <= mid, r, r - mid)
    angle = 2.0 * np.pi / n * ((k[:, None] * r[None, :]) % n)
    scale = np.where((r == 0) | (r == mid), math.sqrt(1.0 / n), math.sqrt(2.0 / n))
    return scale[:, None] * np.where((r <= mid)[:, None], np.cos(angle), np.sin(angle))


def basis_slope_np(n):
    slope = basis_np(n) @ derivative_np(n, n // 2 - 1)
    slope[0] = 0.0
    slope[n // 2] = 0.0
    return slope


def hi_lo(table):
    table = np.asarray(table, np.float32)
    hi = table.astype(bf16)
    lo = (table - hi.astype(np.float32)).astype(bf16)
    return np.stack([hi, lo])


def by_parity(table):
    mid = table.shape[0] // 2
    even = list(range(0, mid + 1, 2)) + list(range(mid + 2, 2 * mid, 2))
    odd = list(range(1, mid, 2)) + list(range(mid + 1, 2 * mid, 2))
    return np.stack([table[even][:, :mid], table[odd][:, :mid]])


def stacked(halves):
    return np.stack([np.concatenate(list(hi_lo(half))) for half in halves])


def dot(a, b):
    return jnp.dot(a, b, preferred_element_type=f32)


def split(x):
    hi = x.astype(bf16)
    return hi, (x - hi.astype(f32)).astype(bf16)


def half3(t_ref, h, x):
    mid = x.shape[0]
    hi, lo = split(x)
    both = dot(t_ref[h], hi)
    return both[:mid] + (both[mid:] + dot(t_ref[h, :mid, :], lo))


def fore3(t_ref, x):
    mid = x.shape[0] // 2
    low, high = x[:mid], x[mid:]
    even = half3(t_ref, 0, low + high)
    odd = half3(t_ref, 1, low - high)
    return jnp.concatenate([even, odd], axis=0)


def back3(t_ref, x):
    mid = x.shape[0] // 2
    even = half3(t_ref, 0, x[:mid])
    odd = half3(t_ref, 1, x[mid:])
    return jnp.concatenate([even + odd, even - odd], axis=0)


def right3(x, t_ref):
    hi, lo = split(x)
    return dot(hi, t_ref[0]) + (dot(hi, t_ref[1]) + dot(lo, t_ref[0]))


def wave_gap(row, length):
    mid = length // 2
    k = jnp.where(row < mid, row, jnp.where(row == mid, 0, row - mid)).astype(f32)
    scaled = (2.0 * math.pi / (length * cell_width)) * k
    return scaled * scaled


def parity_gap(row, length):
    mid = length // 2
    odd = row >= mid
    place = row - jnp.where(odd, mid, 0)
    place = place - jnp.where(place < mid // 2, 0, mid // 2)
    k = (2 * place + jnp.where(odd, 1, 0)).astype(f32)
    scaled = (2.0 * math.pi / (length * cell_width)) * k
    return scaled * scaled


def tile_gap(first_a, first_b, rows, lanes, nx, ny):
    a = first_a + lax.broadcasted_iota(jnp.int32, (rows, lanes), 0)
    b = first_b + lax.broadcasted_iota(jnp.int32, (rows, lanes), 1)
    return parity_gap(a, nx) + wave_gap(b, ny)


def interior_inverse(mu, is_last):
    det = mu * (mu * mu - 2.0)
    lid = mu * mu * (mu - 1.0) - 2.0 * mu + 1.0
    recip = 1.0 / jnp.where(is_last, lid, det)
    m1 = mu - 1.0
    q11 = jnp.where(is_last, mu * m1 - 1.0, mu * mu - 1.0) * recip
    q12 = jnp.where(is_last, m1, mu) * recip
    q13 = recip
    q22 = jnp.where(is_last, mu * m1, mu * mu) * recip
    q23 = mu * recip
    q33 = (mu * mu - 1.0) * recip
    return q11, q12, q13, q22, q23, q33


def thirds(x):
    high = x.astype(bf16)
    rest = x - high.astype(f32)
    middle = rest.astype(bf16)
    return high, middle, (rest - middle.astype(f32)).astype(bf16)


def remote(src, dst, send_sem, recv_sem, to):
    return pltpu.make_async_remote_copy(
        src_ref=src,
        dst_ref=dst,
        send_sem=send_sem,
        recv_sem=recv_sem,
        device_id=to,
        device_id_type=pl.DeviceIdType.MESH,
    )


def stage_kernel(second, *refs):
    refs = list(refs)
    idx_ref = refs.pop(0)
    if second:
        own, other, vin, old, by_b, byd_b, bx_b, bxd_b = refs[:8]
        refs = refs[8:]
    else:
        raw = refs.pop(0)
    tables = refs[:8]
    vout, keep, recv = refs[8:11]
    refs = refs[11:]
    if second:
        now, sent, press = refs[:3]
        raw = sent
        refs = refs[3:]
    else:
        now, pivots, sent = refs[:3]
        local_tables = refs[3:11]
        load_sem = refs[11]
        refs = refs[12:]
        loads = [pltpu.make_async_copy(raw, sent, load_sem.at[0])]
        for i, (source, target) in enumerate(zip(tables, local_tables)):
            loads.append(pltpu.make_async_copy(source, target, load_sem.at[i + 1]))
        for load in loads:
            load.start()
        tables = local_tables
    mask, visc, dlx, dly, by, byd, bx, bxd = tables
    part, halo, spec, work, frp, fr, side, pick, covered, hs, hr, fs, fr_sem, xs, xr = refs
    _, _, nx, ny = now.shape
    fringe = fr.shape[2]
    sec = lax.axis_index("sec")
    me = lax.axis_index("gz")
    slabs = lax.axis_size("gz")
    is_farm = sec == 1
    core = lax.rem(me, 2)
    half = nx // 2
    has_below = (me > 0).astype(f32)
    has_above = (me < slabs - 1).astype(f32)

    out_level, in_level = core, 1 - core
    far = lax.rem(me + 2 * core - 1 + slabs, slabs)
    near = me + 1 - 2 * core
    has_far = jnp.where(core == 0, has_below, has_above)
    lid = jnp.where(core == 0, 1.0, has_above).astype(f32)

    barrier = pltpu.get_barrier_semaphore()
    for to in (
        {"sec": sec, "gz": far},
        {"sec": sec, "gz": near},
        {"sec": 1 - sec, "gz": me},
        {"sec": 1 - sec, "gz": far},
    ):
        pl.semaphore_signal(
            barrier, inc=1, device_id=to, device_id_type=pl.DeviceIdType.MESH
        )
    pl.semaphore_wait(barrier, 4)

    def far_face(c):
        to = {"sec": sec, "gz": far}
        return remote(raw.at[c, out_level], halo.at[0, c], hs.at[0, c], hr.at[0, c], to)

    def near_face(c):
        to = {"sec": sec, "gz": near}
        return remote(now.at[c, in_level], halo.at[1, c], hs.at[1, c], hr.at[1, c], to)

    def columns(i):
        farm = 1 - sec
        if i == 0:
            return remote(frp, fr, fs.at[0], fr_sem.at[0], {"sec": farm, "gz": me})
        return remote(frp.at[out_level], side, fs.at[1], fr_sem.at[1], {"sec": farm, "gz": far})

    def trade(field):
        rows = pl.ds(pl.multiple_of((1 - core) * half, half), half)
        to = {"sec": sec, "gz": near}
        return remote(spec.at[field, rows, :], recv.at[field], xs.at[field], xr.at[field], to)

    def project(c, z):
        p = press[z]
        if c == 0:
            raw[c, z] = vin[c, z] - right3(back3(bxd_b, p), by_b)
        elif c == 1:
            raw[c, z] = vin[c, z] - right3(back3(bx_b, p), byd_b)
        else:
            raw[c, z] = vin[c, z] - right3(back3(bx_b, press[z + 1] - p), by_b)

    order = (2, 1, 0)
    if second:
        press[:, pl.ds(pl.multiple_of(core * half, half), half), :] = own[...]
        press[:, pl.ds(pl.multiple_of((1 - core) * half, half), half), :] = other[...]
        project(order[0], out_level)
    far_face(order[0]).start()
    if second:
        project(order[1], out_level)
        project(order[2], out_level)

        @pl.when(is_farm)
        def _():
            far_face(order[1]).start()
            far_face(order[2]).start()

        for c in order:
            project(c, in_level)

    if not second:
        loads[0].wait()

    @pl.when(jnp.logical_not(is_farm))
    def _():
        place = lax.broadcasted_iota(jnp.int32, (fringe, 1), 0)
        tall = jnp.full((fringe, 1), -1, jnp.int32)
        for f in range(fringe):
            tall = jnp.where(place == f, idx_ref[f], tall)
        hit = lax.broadcasted_iota(jnp.int32, (fringe, nx), 1) == tall
        hit = hit.astype(f32).astype(bf16)
        for z in range(2):
            for c in range(3):
                high, middle, low = thirds(sent[c, z])
                frp[z, c] = (dot(hit, high) + dot(hit, middle)) + dot(hit, low)
        columns(0).start()
        columns(1).start()
        if second:
            far_face(order[1]).start()
            far_face(order[2]).start()

    if not second:
        for c in order[1:]:
            far_face(c).start()
        pivot_table(nx, ny, slabs // 2, pivots)

    def placed(rows, here):
        high, middle, low = thirds(rows)
        stack = jnp.concatenate([high, middle, low, jnp.zeros_like(low)], axis=0)
        return jnp.where(covered[...] > 0.5, dot(pick[...], stack), here)

    @pl.when(is_farm)
    def _():
        lane = lax.broadcasted_iota(jnp.int32, (1, 4 * fringe), 1)
        wide = jnp.full((1, 4 * fringe), -1, jnp.int32)
        for f in range(fringe):
            here = (lane == f) | (lane == f + fringe) | (lane == f + 2 * fringe)
            wide = jnp.where(here, idx_ref[f], wide)
        hit = lax.broadcasted_iota(jnp.int32, (nx, 4 * fringe), 0) == wide
        pick[...] = hit.astype(f32).astype(bf16)
        ones = jnp.ones((fringe, ny), f32)
        ones = jnp.concatenate([ones, jnp.zeros((3 * fringe, ny), f32)], axis=0)
        covered[...] = dot(pick[...], ones.astype(bf16))
        columns(0).wait_recv()
        for z in range(2):
            for c in range(3):
                now[c, z] = placed(fr[z, c], sent[c, z])

    @pl.when(jnp.logical_not(is_farm))
    def _():
        now[...] = sent[...]

    for c in order:
        near_face(c).start()

    if not second:
        for load in loads[1:]:
            load.wait()
    coef = jnp.where(is_farm, drag_coef, 0.0).astype(f32)
    for z in range(2):
        u = now[0, z]
        v = now[1, z]
        drag = coef * mask[z].astype(f32) * jnp.abs(u)
        for c in range(3):
            here = now[c, z]
            r = here.astype(bf16)
            part[c, z] = -(u * dot(dlx[...], r) + v * dot(r, dly[...])) - drag * here

    def update(c, z, beyond, edge):
        here = now[c, z]
        inner = now[c, 1 - z]
        side_sign = (2 * z - 1).astype(f32)
        tend = part[c, z] - now[2, z] * ((0.5 * side_sign) * (beyond - inner))
        tend = tend + visc[z] * (beyond - 2.0 * here + inner)
        if second:
            new = 0.5 * (old[c, z] + here + step_size * tend)
        else:
            new = here + step_size * tend
        if c == 2 and edge:
            new = new * lid
        vout[c, z] = new
        return new

    for c in order:
        near_face(c).wait_recv()
        new = update(c, in_level, halo[1, c], False)
        if c == 2:
            work[1] = right3(new, by)
        elif c == 1:
            spec[in_level] = right3(new, byd)
        else:
            spec[2] = right3(new, by)

    @pl.when(is_farm)
    def _():
        columns(1).wait_recv()

    for c in order:
        far_face(c).wait_recv()

        @pl.when(is_farm)
        def _():
            work[0] = placed(side[c], halo[0, c])

        @pl.when(jnp.logical_not(is_farm))
        def _():
            work[0] = halo[0, c]

        new = update(c, out_level, work[0] * has_far, True)
        if c == 2:
            w_out = right3(new, by)
            w_in = work[1]
            spec[out_level] = w_out - jnp.where(core == 1, w_in, 0.0)
            w_in = w_in - jnp.where(core == 0, w_out, 0.0)
            spec[in_level] = fore3(bx, spec[in_level] + w_in) + fore3(bxd, spec[2])
            trade(in_level).start()
            spec[2] = fore3(bx, jnp.where(core == 0, work[1], w_out))
            trade(2).start()
        elif c == 1:
            spec[out_level] = fore3(bx, spec[out_level] + right3(new, byd))
        else:
            spec[out_level] = spec[out_level] + fore3(bxd, right3(new, by))
            trade(out_level).start()
    keep[...] = spec[:, pl.ds(pl.multiple_of(core * half, half), half), :]
    for field in range(3):
        trade(field).wait()
    for c in range(3):
        far_face(c).wait_send()
        near_face(c).wait_send()

    @pl.when(jnp.logical_not(is_farm))
    def _():
        columns(0).wait_send()
        columns(1).wait_send()


def sources(core, keep, recv, rows):
    first = core == 0

    def pick(field, low):
        own, other = keep[field, rows, :], recv[field, rows, :]
        return jnp.where(first == low, own, other)

    s1 = pick(1, True)
    s2 = pick(0, False) - pick(2, True)
    s3 = pick(1, False)
    return pick, s1, s2, s3


def own_gap(nx, ny):
    me = lax.axis_index("gz")
    core = lax.rem(me, 2)
    chip = lax.div(me, 2)
    lane_blocks = ny // 128
    first_a = core * (nx // 2) + lax.div(chip, lane_blocks) * 8
    first_b = lax.rem(chip, lane_blocks) * 128
    return tile_gap(first_a, first_b, 8, 128, nx, ny)


def pivot_table(nx, ny, chips, pivots):
    eps = own_gap(nx, ny)
    mu = 2.0 + eps
    mm = mu * mu
    inner = mm * eps * (4.0 + eps)
    lid = mm * (mu - 1.0) - 2.0 * mu + 1.0
    last = mu * eps * (mm * mm * (mu + 1.0) - mm * (4.0 * mu + 3.0) + 3.0 * mu + 1.0) / lid
    e = mu * eps * (mm + mu - 1.0)
    pivot = 1.0 / (1.0 + e)
    pivots[0] = pivot

    def body(j, carry):
        e, pivot = carry
        e = inner + e * pivot
        pivot = 1.0 / (1.0 + e)
        pivots[j] = pivot
        return e, pivot

    e, pivot = lax.fori_loop(1, chips - 1, body, (e, pivot))
    e = last + e * pivot
    pivots[chips - 1] = jnp.where(e > 0.0, 1.0 / jnp.where(e > 0.0, e, 1.0), 0.0)


def solve_kernel(
    nx, ny, chips, keep, recv, pivots, own, other, fore, fore_in, back, back_in, work, out, ss, rs
):
    me = lax.axis_index("gz")
    core = lax.rem(me, 2)
    chip = lax.div(me, 2)
    is_last = chip == chips - 1
    half = keep.shape[1]
    lane_blocks = ny // 128
    row_blocks = half // 8
    pieces = 4
    mesh_id = pl.DeviceIdType.MESH
    sibling = {"gz": chip * 2 + (1 - core)}

    def peer(d):
        return {"gz": d * 2 + core}

    def push(src, dst, lane, to):
        return remote(src, dst, ss.at[lane], rs.at[lane], to)

    barrier = pltpu.get_barrier_semaphore()
    pl.semaphore_signal(barrier, inc=1, device_id=sibling, device_id_type=mesh_id)

    def greet(s, carry):
        to = peer(lax.rem(chip + s, chips))
        pl.semaphore_signal(barrier, inc=1, device_id=to, device_id_type=mesh_id)
        return carry

    lax.fori_loop(1, chips, greet, 0)

    def reduce(s, carry):
        rb = lax.rem(lax.div(chip, lane_blocks) + s, row_blocks)
        rows = pl.ds(pl.multiple_of(rb * 8, 8), 8)
        pick, s1, s2, s3 = sources(core, keep, recv, rows)
        mu = 2.0 + tile_gap(core * half + rb * 8, 0, 8, ny, nx, ny)
        q11, q12, q13, q22, q23, q33 = interior_inverse(mu, is_last)
        a = -pick(0, True) - (q11 * s1 + q12 * s2 + q13 * s3)
        c = pick(2, False) - (q13 * s1 + q23 * s2 + q33 * s3)
        for lb in range(lane_blocks):
            fore[rb * lane_blocks + lb, 0] = a[:, lb * 128 : (lb + 1) * 128]
            fore[rb * lane_blocks + lb, 1] = c[:, lb * 128 : (lb + 1) * 128]
        return carry

    lax.fori_loop(0, row_blocks, reduce, 0)
    pl.semaphore_wait(barrier, chips)

    def scatter(source, target, lane):
        def send(s, carry):
            d = lax.rem(chip + s, chips)
            push(source.at[d], target.at[chip], lane, peer(d)).start()
            return carry

        lax.fori_loop(1, chips, send, 0)
        target[chip] = source[chip]
        most = pl.ds(0, chips - 1)
        everything = push(source.at[most], target.at[most], lane, sibling)
        everything.wait_recv()
        return everything

    fore_sent = scatter(fore, fore_in, 1)

    mu = 2.0 + own_gap(nx, ny)
    det = mu * (mu * mu - 2.0)
    y = det * fore_in[0, 0] * pivots[0]
    work[0] = y
    for j in range(1, chips):
        y = (det * (fore_in[j, 0] + fore_in[j - 1, 1]) + y) * pivots[j]
        work[j] = y
    back[chips - 1, 0] = y
    back[chips - 1, 1] = jnp.zeros_like(y)
    for j in range(chips - 2, -1, -1):
        back[j, 1] = y
        y = work[j] + y * pivots[j]
        back[j, 0] = y

    back_sent = scatter(back, back_in, 2)

    def expand(rb, carry):
        rows = pl.ds(pl.multiple_of(rb * 8, 8), 8)
        _, s1, s2, s3 = sources(core, keep, recv, rows)
        mu = 2.0 + tile_gap(core * half + rb * 8, 0, 8, ny, nx, ny)
        q11, q12, q13, q22, q23, q33 = interior_inverse(mu, is_last)
        cols = range(lane_blocks)
        p0 = jnp.concatenate([back_in[rb * lane_blocks + lb, 0] for lb in cols], axis=1)
        p4 = jnp.concatenate([back_in[rb * lane_blocks + lb, 1] for lb in cols], axis=1)
        s1 = s1 - p0
        s3 = s3 - p4
        p1 = -(q11 * s1 + q12 * s2 + q13 * s3)
        p2 = -(q12 * s1 + q22 * s2 + q23 * s3)
        p3 = -(q13 * s1 + q23 * s2 + q33 * s3)
        p4 = jnp.where(is_last, p3, p4)
        first = core == 0
        for field, (low, high) in enumerate(((p0, p2), (p1, p3), (p2, p4))):
            own[field, rows, :] = jnp.where(first, low, high)
            out[field, rows, :] = jnp.where(first, high, low)
        return carry

    step = row_blocks // pieces
    for piece in range(pieces):
        lax.fori_loop(piece * step, (piece + 1) * step, expand, 0)
        rows = pl.ds(piece * step * 8, step * 8)
        push(out.at[:, rows, :], other.at[:, rows, :], 0, sibling).start()
    push(out, other, 0, sibling).wait()
    fore_sent.wait_send()
    back_sent.wait_send()


def backward_kernel(own, other, vin, by, byd, bx, bxd, out, press, new, sems):
    half = own.shape[1]
    core = lax.rem(lax.axis_index("gz"), 2)
    press[:, pl.ds(pl.multiple_of(core * half, half), half), :] = own[...]
    press[:, pl.ds(pl.multiple_of((1 - core) * half, half), half), :] = other[...]
    copies = []

    def finish(c, z, correction):
        new[c, z] = vin[c, z] - correction
        copies.append(pltpu.make_async_copy(new.at[c, z], out.at[c, z], sems.at[c, z]))
        copies[-1].start()

    for z in range(2):
        p = press[z]
        lift = press[z + 1] - p
        finish(0, z, right3(back3(bxd, p), by))
        finish(1, z, right3(back3(bx, p), byd))
        finish(2, z, right3(back3(bx, lift), by))
    for copy in copies:
        copy.wait()


VM = pl.BlockSpec(memory_space=pltpu.VMEM)
SM = pl.BlockSpec(memory_space=pltpu.SMEM)
HB = pl.BlockSpec(memory_space=pltpu.HBM)


def shape(*dims):
    return jax.ShapeDtypeStruct(dims, f32)


def call(kernel, ins, outs, scratch=(), limit=40, flops=0, collective=None, specs=None, to=VM):
    many = isinstance(outs, (list, tuple))
    moved = sum(x.size * x.dtype.itemsize for x in ins)
    moved += sum(math.prod(o.shape) * 4 for o in (outs if many else [outs]))
    return pl.pallas_call(
        kernel,
        out_shape=outs,
        in_specs=specs or [VM] * len(ins),
        out_specs=[to] * len(outs) if many else to,
        scratch_shapes=[pltpu.VMEM(s, f32) if isinstance(s, tuple) else s for s in scratch],
        compiler_params=pltpu.CompilerParams(
            vmem_limit_bytes=limit * MIB,
            collective_id=collective,
            has_side_effects=collective is not None,
        ),
        cost_estimate=pl.CostEstimate(flops=flops, bytes_accessed=moved, transcendentals=0),
    )(*ins)


def local(velocity, eddy_viscosity, turbine_mask, idx):
    velocity = velocity[0]
    visc = eddy_viscosity[0]
    _, _, nx, ny = velocity.shape
    fringe = idx.shape[0]
    slabs = lax.axis_size("gz")
    chips = slabs // 2
    half = nx // 2
    plane = 2 * nx * ny

    slope_x, slope_y = by_parity(basis_slope_np(nx)), basis_slope_np(ny)
    base_x, base_y = by_parity(basis_np(nx)), basis_np(ny)
    turned = (0, 2, 1)
    dlx = jnp.asarray(derivative_np(nx, (nx - 1) // 3).astype(np.float32).astype(bf16))
    dly = jnp.asarray(derivative_np(ny, (ny - 1) // 3).T.astype(np.float32).astype(bf16))
    fore = [hi_lo(base_y.T), hi_lo(slope_y.T), stacked(base_x), stacked(slope_x)]
    back = [
        hi_lo(base_y),
        hi_lo(-slope_y),
        stacked(base_x.transpose(turned)),
        stacked(-slope_x.transpose(turned)),
    ]
    fore = [jnp.asarray(t) for t in fore]
    back = [jnp.asarray(t) for t in back]
    field = (3, 2, nx, ny)
    dma = pltpu.SemaphoreType.DMA
    stage_out = [shape(*field), shape(3, half, ny), shape(3, half, ny)]
    stage_scratch = [
        field,
        (2, 3, nx, ny),
        (3, nx, ny),
        (2, nx, ny),
        (2, 3, fringe, ny),
        (2, 3, fringe, ny),
        (3, fringe, ny),
        pltpu.VMEM((nx, 4 * fringe), bf16),
        (nx, ny),
        dma((2, 3)),
        dma((2, 3)),
        dma((2,)),
        dma((2,)),
        dma((3,)),
        dma((3,)),
    ]
    shared = [turbine_mask, visc, dlx, dly] + fore
    ahead = plane * (6 * nx + 6 * ny) + 3 * plane * (6 * ny + 5 * nx)

    def solve(keep, recv, pivots):
        column = (chips, 2, 8, 128)
        return call(
            functools.partial(solve_kernel, nx, ny, chips),
            [keep, recv, pivots],
            [shape(3, half, ny), shape(3, half, ny)],
            scratch=[column] * 4 + [(chips, 8, 128), (3, half, ny)] + [dma((3,))] * 2,
            limit=12,
            collective=0,
        )

    loaded = [field] + [pltpu.VMEM(t.shape, t.dtype) for t in shared] + [dma((9,))]
    state, keep, recv, start, pivots = call(
        functools.partial(stage_kernel, False),
        [idx] + [pltpu.with_memory_space_constraint(x, pltpu.HBM) for x in [velocity] + shared],
        stage_out + [shape(*field), shape(chips, 8, 128)],
        scratch=loaded + stage_scratch,
        limit=30,
        flops=ahead,
        collective=1,
        specs=[SM] + [HB] * (1 + len(shared)),
    )
    own, other = solve(keep, recv, pivots)
    state, keep, recv = call(
        functools.partial(stage_kernel, True),
        [idx, own, other, state, start] + back + shared,
        stage_out,
        scratch=[field, field, (3, nx, ny)] + stage_scratch,
        limit=28,
        flops=ahead + 3 * plane * (6 * ny + 6 * nx),
        collective=2,
        specs=[SM] + [VM] * (8 + len(shared)),
    )
    own, other = solve(keep, recv, pivots)
    result = call(
        backward_kernel,
        [own, other, state] + back,
        shape(*field),
        scratch=[(3, nx, ny), field, dma((3, 2))],
        limit=16,
        flops=3 * plane * (6 * ny + 6 * nx),
        to=HB,
    )
    return result[None]


def solution(mesh):
    placed = (
        P("sec", None, "gz", None, None),
        P("sec", "gz", None, None),
        P("gz", None, None),
        P(),
    )
    return jax.shard_map(
        local,
        mesh=mesh,
        in_specs=placed,
        out_specs=P("sec", None, "gz", None, None),
        check_vma=False,
    )
```

```python
import functools
import math

import jax
import jax.numpy as jnp
import numpy as np
from jax import lax
from jax.experimental import pallas as pl
from jax.experimental.pallas import tpu as pltpu
from jax.sharding import PartitionSpec as P

step_size = 0.1
drag_coef = 0.75
cell_width = 4.0
f32 = jnp.float32
bf16 = jnp.bfloat16
MIB = 1024 * 1024


def derivative_np(n, cutoff):
    i = np.arange(n)
    k = np.arange(1, cutoff + 1)
    wave = 2.0 * np.pi * k / n
    shift = np.sin(2.0 * np.pi / n * ((i[:, None] * k[None, :]) % n)) @ wave
    shift = -(2.0 / (cell_width * n)) * shift
    return shift[(i[:, None] - i[None, :]) % n]


def basis_np(n):
    mid = n // 2
    r = np.arange(n)
    k = np.where(r <= mid, r, r - mid)
    angle = 2.0 * np.pi / n * ((k[:, None] * r[None, :]) % n)
    scale = np.where((r == 0) | (r == mid), math.sqrt(1.0 / n), math.sqrt(2.0 / n))
    return scale[:, None] * np.where((r <= mid)[:, None], np.cos(angle), np.sin(angle))


def basis_slope_np(n):
    slope = basis_np(n) @ derivative_np(n, n // 2 - 1)
    slope[0] = 0.0
    slope[n // 2] = 0.0
    return slope


def hi_lo(table):
    table = np.asarray(table, np.float32)
    hi = table.astype(bf16)
    lo = (table - hi.astype(np.float32)).astype(bf16)
    return np.stack([hi, lo])


def by_parity(table):
    mid = table.shape[0] // 2
    even = list(range(0, mid + 1, 2)) + list(range(mid + 2, 2 * mid, 2))
    odd = list(range(1, mid, 2)) + list(range(mid + 1, 2 * mid, 2))
    return np.stack([table[even][:, :mid], table[odd][:, :mid]])


def stacked(halves):
    return np.stack([np.concatenate(list(hi_lo(half))) for half in halves])


def dot(a, b):
    return jnp.dot(a, b, preferred_element_type=f32)


def split(x):
    hi = x.astype(bf16)
    return hi, (x - hi.astype(f32)).astype(bf16)


def half3(t_ref, h, x):
    mid = x.shape[0]
    hi, lo = split(x)
    both = dot(t_ref[h], hi)
    return both[:mid] + (both[mid:] + dot(t_ref[h, :mid, :], lo))


def fore3(t_ref, x):
    mid = x.shape[0] // 2
    low, high = x[:mid], x[mid:]
    even = half3(t_ref, 0, low + high)
    odd = half3(t_ref, 1, low - high)
    return jnp.concatenate([even, odd], axis=0)


def back3(t_ref, x):
    mid = x.shape[0] // 2
    even = half3(t_ref, 0, x[:mid])
    odd = half3(t_ref, 1, x[mid:])
    return jnp.concatenate([even + odd, even - odd], axis=0)


def right3(x, t_ref):
    hi, lo = split(x)
    return dot(hi, t_ref[0]) + (dot(hi, t_ref[1]) + dot(lo, t_ref[0]))


def wave_gap(row, length):
    mid = length // 2
    k = jnp.where(row < mid, row, jnp.where(row == mid, 0, row - mid)).astype(f32)
    scaled = (2.0 * math.pi / (length * cell_width)) * k
    return scaled * scaled


def parity_gap(row, length):
    mid = length // 2
    odd = row >= mid
    place = row - jnp.where(odd, mid, 0)
    place = place - jnp.where(place < mid // 2, 0, mid // 2)
    k = (2 * place + jnp.where(odd, 1, 0)).astype(f32)
    scaled = (2.0 * math.pi / (length * cell_width)) * k
    return scaled * scaled


def tile_gap(first_a, first_b, rows, lanes, nx, ny):
    a = first_a + lax.broadcasted_iota(jnp.int32, (rows, lanes), 0)
    b = first_b + lax.broadcasted_iota(jnp.int32, (rows, lanes), 1)
    return parity_gap(a, nx) + wave_gap(b, ny)


def interior_inverse(mu, is_last):
    det = mu * (mu * mu - 2.0)
    lid = mu * mu * (mu - 1.0) - 2.0 * mu + 1.0
    recip = 1.0 / jnp.where(is_last, lid, det)
    m1 = mu - 1.0
    q11 = jnp.where(is_last, mu * m1 - 1.0, mu * mu - 1.0) * recip
    q12 = jnp.where(is_last, m1, mu) * recip
    q13 = recip
    q22 = jnp.where(is_last, mu * m1, mu * mu) * recip
    q23 = mu * recip
    q33 = (mu * mu - 1.0) * recip
    return q11, q12, q13, q22, q23, q33


def thirds(x):
    high = x.astype(bf16)
    rest = x - high.astype(f32)
    middle = rest.astype(bf16)
    return high, middle, (rest - middle.astype(f32)).astype(bf16)


def remote(src, dst, send_sem, recv_sem, to):
    return pltpu.make_async_remote_copy(
        src_ref=src,
        dst_ref=dst,
        send_sem=send_sem,
        recv_sem=recv_sem,
        device_id=to,
        device_id_type=pl.DeviceIdType.MESH,
    )


def stage_kernel(second, *refs):
    refs = list(refs)
    idx_ref = refs.pop(0)
    if second:
        own, other, vin, old, by_b, byd_b, bx_b, bxd_b = refs[:8]
        refs = refs[8:]
    else:
        raw = refs.pop(0)
    tables = refs[:8]
    vout, keep, recv = refs[8:11]
    refs = refs[11:]
    if second:
        now, sent, press = refs[:3]
        raw = sent
        refs = refs[3:]
    else:
        now, pivots, sent = refs[:3]
        local_tables = refs[3:11]
        load_sem = refs[11]
        refs = refs[12:]
        loads = [pltpu.make_async_copy(raw, sent, load_sem.at[0])]
        for i, (source, target) in enumerate(zip(tables, local_tables)):
            loads.append(pltpu.make_async_copy(source, target, load_sem.at[i + 1]))
        for load in loads:
            load.start()
        tables = local_tables
    mask, visc, dlx, dly, by, byd, bx, bxd = tables
    part, halo, spec, work, frp, fr, side, pick, covered, hs, hr, fs, fr_sem, xs, xr = refs
    _, _, nx, ny = now.shape
    fringe = fr.shape[2]
    sec = lax.axis_index("sec")
    me = lax.axis_index("gz")
    slabs = lax.axis_size("gz")
    is_farm = sec == 1
    core = lax.rem(me, 2)
    half = nx // 2
    has_below = (me > 0).astype(f32)
    has_above = (me < slabs - 1).astype(f32)

    out_level, in_level = core, 1 - core
    far = lax.rem(me + 2 * core - 1 + slabs, slabs)
    near = me + 1 - 2 * core
    has_far = jnp.where(core == 0, has_below, has_above)
    lid = jnp.where(core == 0, 1.0, has_above).astype(f32)

    barrier = pltpu.get_barrier_semaphore()
    for to in (
        {"sec": sec, "gz": far},
        {"sec": sec, "gz": near},
        {"sec": 1 - sec, "gz": me},
        {"sec": 1 - sec, "gz": far},
    ):
        pl.semaphore_signal(
            barrier, inc=1, device_id=to, device_id_type=pl.DeviceIdType.MESH
        )
    pl.semaphore_wait(barrier, 4)

    def far_face(c):
        to = {"sec": sec, "gz": far}
        return remote(raw.at[c, out_level], halo.at[0, c], hs.at[0, c], hr.at[0, c], to)

    def near_face(c):
        to = {"sec": sec, "gz": near}
        return remote(now.at[c, in_level], halo.at[1, c], hs.at[1, c], hr.at[1, c], to)

    def columns(i):
        farm = 1 - sec
        if i == 0:
            return remote(frp, fr, fs.at[0], fr_sem.at[0], {"sec": farm, "gz": me})
        return remote(frp.at[out_level], side, fs.at[1], fr_sem.at[1], {"sec": farm, "gz": far})

    def trade(field):
        rows = pl.ds(pl.multiple_of((1 - core) * half, half), half)
        to = {"sec": sec, "gz": near}
        return remote(spec.at[field, rows, :], recv.at[field], xs.at[field], xr.at[field], to)

    def project(c, z):
        p = press[z]
        if c == 0:
            raw[c, z] = vin[c, z] - right3(back3(bxd_b, p), by_b)
        elif c == 1:
            raw[c, z] = vin[c, z] - right3(back3(bx_b, p), byd_b)
        else:
            raw[c, z] = vin[c, z] - right3(back3(bx_b, press[z + 1] - p), by_b)

    order = (2, 1, 0)
    if second:
        press[:, pl.ds(pl.multiple_of(core * half, half), half), :] = own[...]
        press[:, pl.ds(pl.multiple_of((1 - core) * half, half), half), :] = other[...]
        project(order[0], out_level)
    far_face(order[0]).start()
    if second:
        project(order[1], out_level)
        project(order[2], out_level)

        @pl.when(is_farm)
        def _():
            far_face(order[1]).start()
            far_face(order[2]).start()

        for c in order:
            project(c, in_level)

    if not second:
        loads[0].wait()

    @pl.when(jnp.logical_not(is_farm))
    def _():
        place = lax.broadcasted_iota(jnp.int32, (fringe, 1), 0)
        tall = jnp.full((fringe, 1), -1, jnp.int32)
        for f in range(fringe):
            tall = jnp.where(place == f, idx_ref[f], tall)
        hit = lax.broadcasted_iota(jnp.int32, (fringe, nx), 1) == tall
        hit = hit.astype(f32).astype(bf16)
        for z in range(2):
            for c in range(3):
                high, middle, low = thirds(sent[c, z])
                frp[z, c] = (dot(hit, high) + dot(hit, middle)) + dot(hit, low)
        columns(0).start()
        columns(1).start()
        if second:
            far_face(order[1]).start()
            far_face(order[2]).start()

    if not second:
        for c in order[1:]:
            far_face(c).start()
        pivot_table(nx, ny, slabs // 2, pivots)

    def placed(rows, here):
        high, middle, low = thirds(rows)
        stack = jnp.concatenate([high, middle, low, jnp.zeros_like(low)], axis=0)
        return jnp.where(covered[...] > 0.5, dot(pick[...], stack), here)

    @pl.when(is_farm)
    def _():
        lane = lax.broadcasted_iota(jnp.int32, (1, 4 * fringe), 1)
        wide = jnp.full((1, 4 * fringe), -1, jnp.int32)
        for f in range(fringe):
            here = (lane == f) | (lane == f + fringe) | (lane == f + 2 * fringe)
            wide = jnp.where(here, idx_ref[f], wide)
        hit = lax.broadcasted_iota(jnp.int32, (nx, 4 * fringe), 0) == wide
        pick[...] = hit.astype(f32).astype(bf16)
        ones = jnp.ones((fringe, ny), f32)
        ones = jnp.concatenate([ones, jnp.zeros((3 * fringe, ny), f32)], axis=0)
        covered[...] = dot(pick[...], ones.astype(bf16))
        columns(0).wait_recv()
        for z in range(2):
            for c in range(3):
                now[c, z] = placed(fr[z, c], sent[c, z])

    @pl.when(jnp.logical_not(is_farm))
    def _():
        now[...] = sent[...]

    for c in order:
        near_face(c).start()

    if not second:
        for load in loads[1:]:
            load.wait()
    coef = jnp.where(is_farm, drag_coef, 0.0).astype(f32)
    for z in range(2):
        u = now[0, z]
        v = now[1, z]
        drag = coef * mask[z].astype(f32) * jnp.abs(u)
        for c in range(3):
            here = now[c, z]
            r = here.astype(bf16)
            part[c, z] = -(u * dot(dlx[...], r) + v * dot(r, dly[...])) - drag * here

    def update(c, z, beyond, edge):
        here = now[c, z]
        inner = now[c, 1 - z]
        side_sign = (2 * z - 1).astype(f32)
        tend = part[c, z] - now[2, z] * ((0.5 * side_sign) * (beyond - inner))
        tend = tend + visc[z] * (beyond - 2.0 * here + inner)
        if second:
            new = 0.5 * (old[c, z] + here + step_size * tend)
        else:
            new = here + step_size * tend
        if c == 2 and edge:
            new = new * lid
        vout[c, z] = new
        return new

    for c in order:
        near_face(c).wait_recv()
        new = update(c, in_level, halo[1, c], False)
        if c == 2:
            work[1] = right3(new, by)
        elif c == 1:
            spec[in_level] = right3(new, byd)
        else:
            spec[2] = right3(new, by)

    @pl.when(is_farm)
    def _():
        columns(1).wait_recv()

    for c in order:
        far_face(c).wait_recv()

        @pl.when(is_farm)
        def _():
            work[0] = placed(side[c], halo[0, c])

        @pl.when(jnp.logical_not(is_farm))
        def _():
            work[0] = halo[0, c]

        new = update(c, out_level, work[0] * has_far, True)
        if c == 2:
            w_out = right3(new, by)
            w_in = work[1]
            spec[out_level] = w_out - jnp.where(core == 1, w_in, 0.0)
            w_in = w_in - jnp.where(core == 0, w_out, 0.0)
            spec[in_level] = fore3(bx, spec[in_level] + w_in) + fore3(bxd, spec[2])
            trade(in_level).start()
            spec[2] = fore3(bx, jnp.where(core == 0, work[1], w_out))
            trade(2).start()
        elif c == 1:
            spec[out_level] = fore3(bx, spec[out_level] + right3(new, byd))
        else:
            spec[out_level] = spec[out_level] + fore3(bxd, right3(new, by))
            trade(out_level).start()
    keep[...] = spec[:, pl.ds(pl.multiple_of(core * half, half), half), :]
    for field in range(3):
        trade(field).wait()
    for c in range(3):
        far_face(c).wait_send()
        near_face(c).wait_send()

    @pl.when(jnp.logical_not(is_farm))
    def _():
        columns(0).wait_send()
        columns(1).wait_send()


def sources(core, keep, recv, rows):
    first = core == 0

    def pick(field, low):
        own, other = keep[field, rows, :], recv[field, rows, :]
        return jnp.where(first == low, own, other)

    s1 = pick(1, True)
    s2 = pick(0, False) - pick(2, True)
    s3 = pick(1, False)
    return pick, s1, s2, s3


def own_gap(h, nx, ny):
    me = lax.axis_index("gz")
    core = lax.rem(me, 2)
    chip = lax.div(me, 2)
    lane_blocks = ny // 128
    place = lax.broadcasted_iota(jnp.int32, (8, 128), 0)
    place = jnp.where(place < 4, place, place - 4)
    a = core * (nx // 2) + lax.div(chip, lane_blocks) * 8 + 4 * h + place
    b = lax.rem(chip, lane_blocks) * 128 + lax.broadcasted_iota(jnp.int32, (8, 128), 1)
    return parity_gap(a, nx) + wave_gap(b, ny)


def pivot_table(nx, ny, chips, pivots):
    for h in range(2):
        eps = own_gap(h, nx, ny)
        mu = 2.0 + eps
        mm = mu * mu
        inner = mm * eps * (4.0 + eps)
        lid = mm * (mu - 1.0) - 2.0 * mu + 1.0
        last = mu * eps * (mm * mm * (mu + 1.0) - mm * (4.0 * mu + 3.0) + 3.0 * mu + 1.0) / lid
        e = mu * eps * (mm + mu - 1.0)
        pivot = 1.0 / (1.0 + e)
        pivots[h, 0] = pivot

        def body(j, carry):
            e, pivot = carry
            e = inner + e * pivot
            pivot = 1.0 / (1.0 + e)
            pivots[h, j] = pivot
            return e, pivot

        e, pivot = lax.fori_loop(1, chips - 1, body, (e, pivot))
        e = last + e * pivot
        pivots[h, chips - 1] = jnp.where(e > 0.0, 1.0 / jnp.where(e > 0.0, e, 1.0), 0.0)


def solve_kernel(
    nx, ny, chips, keep, recv, pivots, own, other, fore, fore_in, back, back_in, work, out, ss, rs
):
    me = lax.axis_index("gz")
    core = lax.rem(me, 2)
    chip = lax.div(me, 2)
    is_last = chip == chips - 1
    half = keep.shape[1]
    lane_blocks = ny // 128
    row_blocks = half // 8
    pieces = 4
    mesh_id = pl.DeviceIdType.MESH
    sibling = {"gz": chip * 2 + (1 - core)}

    def peer(d):
        return {"gz": d * 2 + core}

    def push(src, dst, lane, to):
        return remote(src, dst, ss.at[lane], rs.at[lane], to)

    barrier = pltpu.get_barrier_semaphore()
    pl.semaphore_signal(barrier, inc=1, device_id=sibling, device_id_type=mesh_id)

    def greet(s, carry):
        to = peer(lax.rem(chip + s, chips))
        pl.semaphore_signal(barrier, inc=1, device_id=to, device_id_type=mesh_id)
        return carry

    lax.fori_loop(1, chips, greet, 0)

    def reduce(s, carry):
        rb = lax.rem(lax.div(chip, lane_blocks) + s, row_blocks)
        rows = pl.ds(pl.multiple_of(rb * 8, 8), 8)
        pick, s1, s2, s3 = sources(core, keep, recv, rows)
        mu = 2.0 + tile_gap(core * half + rb * 8, 0, 8, ny, nx, ny)
        q11, q12, q13, q22, q23, q33 = interior_inverse(mu, is_last)
        a = -pick(0, True) - (q11 * s1 + q12 * s2 + q13 * s3)
        c = pick(2, False) - (q13 * s1 + q23 * s2 + q33 * s3)
        for lb in range(lane_blocks):
            lanes = slice(lb * 128, (lb + 1) * 128)
            for h in range(2):
                rows4 = slice(4 * h, 4 * h + 4)
                pair = [a[rows4, lanes], c[rows4, lanes]]
                fore[h, rb * lane_blocks + lb] = jnp.concatenate(pair, axis=0)
        return carry

    lax.fori_loop(0, row_blocks, reduce, 0)
    pl.semaphore_wait(barrier, chips)

    def scatter(source, target, lane):
        def send(s, carry):
            d = lax.rem(chip + s, chips)
            push(source.at[d], target.at[chip], lane, peer(d)).start()
            return carry

        lax.fori_loop(1, chips, send, 0)
        target[chip] = source[chip]
        most = pl.ds(0, chips - 1)
        return push(source.at[most], target.at[most], lane, sibling)

    low = lax.broadcasted_iota(jnp.int32, (8, 128), 0) < 4

    def column(h):
        mu = 2.0 + own_gap(h, nx, ny)
        det = mu * (mu * mu - 2.0)
        tile = fore_in[h, 0]
        turned = pltpu.roll(tile, 4, 0)
        y = det * jnp.where(low, tile, turned) * pivots[h, 0]
        work[0] = y
        for j in range(1, chips):
            carry = jnp.where(low, turned, tile)
            tile = fore_in[h, j]
            turned = pltpu.roll(tile, 4, 0)
            y = (det * (jnp.where(low, tile, turned) + carry) + y) * pivots[h, j]
            work[j] = y
        back[h, chips - 1] = jnp.where(low, y, 0.0)
        for j in range(chips - 2, -1, -1):
            above = y
            y = work[j] + y * pivots[h, j]
            back[h, j] = jnp.where(low, y, above)

    trips = [scatter(fore.at[h], fore_in.at[h], 1 + h) for h in range(2)]
    for h in range(2):
        trips[h].wait_recv()
        column(h)
        trips.append(scatter(back.at[h], back_in.at[h], 3 + h))
    for h in range(2):
        trips[2 + h].wait_recv()

    def expand(rb, carry):
        rows = pl.ds(pl.multiple_of(rb * 8, 8), 8)
        _, s1, s2, s3 = sources(core, keep, recv, rows)
        mu = 2.0 + tile_gap(core * half + rb * 8, 0, 8, ny, nx, ny)
        q11, q12, q13, q22, q23, q33 = interior_inverse(mu, is_last)
        cols = range(lane_blocks)
        top = jnp.concatenate([back_in[0, rb * lane_blocks + lb] for lb in cols], axis=1)
        bottom = jnp.concatenate([back_in[1, rb * lane_blocks + lb] for lb in cols], axis=1)
        p0 = jnp.concatenate([top[:4], bottom[:4]], axis=0)
        p4 = jnp.concatenate([top[4:], bottom[4:]], axis=0)
        s1 = s1 - p0
        s3 = s3 - p4
        p1 = -(q11 * s1 + q12 * s2 + q13 * s3)
        p2 = -(q12 * s1 + q22 * s2 + q23 * s3)
        p3 = -(q13 * s1 + q23 * s2 + q33 * s3)
        p4 = jnp.where(is_last, p3, p4)
        first = core == 0
        for field, (low, high) in enumerate(((p0, p2), (p1, p3), (p2, p4))):
            own[field, rows, :] = jnp.where(first, low, high)
            out[field, rows, :] = jnp.where(first, high, low)
        return carry

    step = row_blocks // pieces
    for piece in range(pieces):
        lax.fori_loop(piece * step, (piece + 1) * step, expand, 0)
        rows = pl.ds(piece * step * 8, step * 8)
        push(out.at[:, rows, :], other.at[:, rows, :], 0, sibling).start()
    push(out, other, 0, sibling).wait()
    for trip in trips:
        trip.wait_send()


def backward_kernel(own, other, vin, by, byd, bx, bxd, out, press, new, sems):
    half = own.shape[1]
    core = lax.rem(lax.axis_index("gz"), 2)
    press[:, pl.ds(pl.multiple_of(core * half, half), half), :] = own[...]
    press[:, pl.ds(pl.multiple_of((1 - core) * half, half), half), :] = other[...]
    copies = []

    def finish(c, z, correction):
        new[c, z] = vin[c, z] - correction
        copies.append(pltpu.make_async_copy(new.at[c, z], out.at[c, z], sems.at[c, z]))
        copies[-1].start()

    for z in range(2):
        p = press[z]
        lift = press[z + 1] - p
        finish(0, z, right3(back3(bxd, p), by))
        finish(1, z, right3(back3(bx, p), byd))
        finish(2, z, right3(back3(bx, lift), by))
    for copy in copies:
        copy.wait()


VM = pl.BlockSpec(memory_space=pltpu.VMEM)
SM = pl.BlockSpec(memory_space=pltpu.SMEM)
HB = pl.BlockSpec(memory_space=pltpu.HBM)


def shape(*dims):
    return jax.ShapeDtypeStruct(dims, f32)


def call(kernel, ins, outs, scratch=(), limit=40, flops=0, collective=None, specs=None, to=VM):
    many = isinstance(outs, (list, tuple))
    moved = sum(x.size * x.dtype.itemsize for x in ins)
    moved += sum(math.prod(o.shape) * 4 for o in (outs if many else [outs]))
    return pl.pallas_call(
        kernel,
        out_shape=outs,
        in_specs=specs or [VM] * len(ins),
        out_specs=[to] * len(outs) if many else to,
        scratch_shapes=[pltpu.VMEM(s, f32) if isinstance(s, tuple) else s for s in scratch],
        compiler_params=pltpu.CompilerParams(
            vmem_limit_bytes=limit * MIB,
            collective_id=collective,
            has_side_effects=collective is not None,
        ),
        cost_estimate=pl.CostEstimate(flops=flops, bytes_accessed=moved, transcendentals=0),
    )(*ins)


def local(velocity, eddy_viscosity, turbine_mask, idx):
    velocity = velocity[0]
    visc = eddy_viscosity[0]
    _, _, nx, ny = velocity.shape
    fringe = idx.shape[0]
    slabs = lax.axis_size("gz")
    chips = slabs // 2
    half = nx // 2
    plane = 2 * nx * ny

    slope_x, slope_y = by_parity(basis_slope_np(nx)), basis_slope_np(ny)
    base_x, base_y = by_parity(basis_np(nx)), basis_np(ny)
    turned = (0, 2, 1)
    dlx = jnp.asarray(derivative_np(nx, (nx - 1) // 3).astype(np.float32).astype(bf16))
    dly = jnp.asarray(derivative_np(ny, (ny - 1) // 3).T.astype(np.float32).astype(bf16))
    fore = [hi_lo(base_y.T), hi_lo(slope_y.T), stacked(base_x), stacked(slope_x)]
    back = [
        hi_lo(base_y),
        hi_lo(-slope_y),
        stacked(base_x.transpose(turned)),
        stacked(-slope_x.transpose(turned)),
    ]
    fore = [jnp.asarray(t) for t in fore]
    back = [jnp.asarray(t) for t in back]
    field = (3, 2, nx, ny)
    dma = pltpu.SemaphoreType.DMA
    stage_out = [shape(*field), shape(3, half, ny), shape(3, half, ny)]
    stage_scratch = [
        field,
        (2, 3, nx, ny),
        (3, nx, ny),
        (2, nx, ny),
        (2, 3, fringe, ny),
        (2, 3, fringe, ny),
        (3, fringe, ny),
        pltpu.VMEM((nx, 4 * fringe), bf16),
        (nx, ny),
        dma((2, 3)),
        dma((2, 3)),
        dma((2,)),
        dma((2,)),
        dma((3,)),
        dma((3,)),
    ]
    shared = [turbine_mask, visc, dlx, dly] + fore
    ahead = plane * (6 * nx + 6 * ny) + 3 * plane * (6 * ny + 5 * nx)

    def solve(keep, recv, pivots):
        column = (2, chips, 8, 128)
        return call(
            functools.partial(solve_kernel, nx, ny, chips),
            [keep, recv, pivots],
            [shape(3, half, ny), shape(3, half, ny)],
            scratch=[column] * 4 + [(chips, 8, 128), (3, half, ny)] + [dma((5,))] * 2,
            limit=12,
            collective=0,
        )

    loaded = [field] + [pltpu.VMEM(t.shape, t.dtype) for t in shared] + [dma((9,))]
    state, keep, recv, start, pivots = call(
        functools.partial(stage_kernel, False),
        [idx] + [pltpu.with_memory_space_constraint(x, pltpu.HBM) for x in [velocity] + shared],
        stage_out + [shape(*field), shape(2, chips, 8, 128)],
        scratch=loaded + stage_scratch,
        limit=30,
        flops=ahead,
        collective=1,
        specs=[SM] + [HB] * (1 + len(shared)),
    )
    own, other = solve(keep, recv, pivots)
    state, keep, recv = call(
        functools.partial(stage_kernel, True),
        [idx, own, other, state, start] + back + shared,
        stage_out,
        scratch=[field, field, (3, nx, ny)] + stage_scratch,
        limit=28,
        flops=ahead + 3 * plane * (6 * ny + 6 * nx),
        collective=2,
        specs=[SM] + [VM] * (8 + len(shared)),
    )
    own, other = solve(keep, recv, pivots)
    result = call(
        backward_kernel,
        [own, other, state] + back,
        shape(*field),
        scratch=[(3, nx, ny), field, dma((3, 2))],
        limit=16,
        flops=3 * plane * (6 * ny + 6 * nx),
        to=HB,
    )
    return result[None]


def solution(mesh):
    placed = (
        P("sec", None, "gz", None, None),
        P("sec", "gz", None, None),
        P("gz", None, None),
        P(),
    )
    return jax.shard_map(
        local,
        mesh=mesh,
        in_specs=placed,
        out_specs=P("sec", None, "gz", None, None),
        check_vma=False,
    )
```

```python
import functools
import math

import jax
import jax.numpy as jnp
import numpy as np
from jax import lax
from jax.experimental import pallas as pl
from jax.experimental.pallas import tpu as pltpu
from jax.sharding import PartitionSpec as P

step_size = 0.1
drag_coef = 0.75
cell_width = 4.0
f32 = jnp.float32
bf16 = jnp.bfloat16
MIB = 1024 * 1024


def derivative_np(n, cutoff):
    i = np.arange(n)
    k = np.arange(1, cutoff + 1)
    wave = 2.0 * np.pi * k / n
    shift = np.sin(2.0 * np.pi / n * ((i[:, None] * k[None, :]) % n)) @ wave
    shift = -(2.0 / (cell_width * n)) * shift
    return shift[(i[:, None] - i[None, :]) % n]


def basis_np(n):
    mid = n // 2
    r = np.arange(n)
    k = np.where(r <= mid, r, r - mid)
    angle = 2.0 * np.pi / n * ((k[:, None] * r[None, :]) % n)
    scale = np.where((r == 0) | (r == mid), math.sqrt(1.0 / n), math.sqrt(2.0 / n))
    return scale[:, None] * np.where((r <= mid)[:, None], np.cos(angle), np.sin(angle))


def basis_slope_np(n):
    slope = basis_np(n) @ derivative_np(n, n // 2 - 1)
    slope[0] = 0.0
    slope[n // 2] = 0.0
    return slope


def hi_lo(table):
    table = np.asarray(table, np.float32)
    hi = table.astype(bf16)
    lo = (table - hi.astype(np.float32)).astype(bf16)
    return np.stack([hi, lo])


def by_parity(table):
    mid = table.shape[0] // 2
    even = list(range(0, mid + 1, 2)) + list(range(mid + 2, 2 * mid, 2))
    odd = list(range(1, mid, 2)) + list(range(mid + 1, 2 * mid, 2))
    return np.stack([table[even][:, :mid], table[odd][:, :mid]])


def stacked(halves):
    return np.stack([np.concatenate(list(hi_lo(half))) for half in halves])


def dot(a, b):
    return jnp.dot(a, b, preferred_element_type=f32)


def split(x):
    hi = x.astype(bf16)
    return hi, (x - hi.astype(f32)).astype(bf16)


def half3(t_ref, h, x):
    mid = x.shape[0]
    hi, lo = split(x)
    both = dot(t_ref[h], hi)
    return both[:mid] + (both[mid:] + dot(t_ref[h, :mid, :], lo))


def fore3(t_ref, x):
    mid = x.shape[0] // 2
    low, high = x[:mid], x[mid:]
    even = half3(t_ref, 0, low + high)
    odd = half3(t_ref, 1, low - high)
    return jnp.concatenate([even, odd], axis=0)


def back3(t_ref, x):
    mid = x.shape[0] // 2
    even = half3(t_ref, 0, x[:mid])
    odd = half3(t_ref, 1, x[mid:])
    return jnp.concatenate([even + odd, even - odd], axis=0)


def right3(x, t_ref):
    hi, lo = split(x)
    return dot(hi, t_ref[0]) + (dot(hi, t_ref[1]) + dot(lo, t_ref[0]))


def wave_gap(row, length):
    mid = length // 2
    k = jnp.where(row < mid, row, jnp.where(row == mid, 0, row - mid)).astype(f32)
    scaled = (2.0 * math.pi / (length * cell_width)) * k
    return scaled * scaled


def parity_gap(row, length):
    mid = length // 2
    odd = row >= mid
    place = row - jnp.where(odd, mid, 0)
    place = place - jnp.where(place < mid // 2, 0, mid // 2)
    k = (2 * place + jnp.where(odd, 1, 0)).astype(f32)
    scaled = (2.0 * math.pi / (length * cell_width)) * k
    return scaled * scaled


def tile_gap(first_a, first_b, rows, lanes, nx, ny):
    a = first_a + lax.broadcasted_iota(jnp.int32, (rows, lanes), 0)
    b = first_b + lax.broadcasted_iota(jnp.int32, (rows, lanes), 1)
    return parity_gap(a, nx) + wave_gap(b, ny)


def interior_inverse(mu, is_last):
    det = mu * (mu * mu - 2.0)
    lid = mu * mu * (mu - 1.0) - 2.0 * mu + 1.0
    recip = 1.0 / jnp.where(is_last, lid, det)
    m1 = mu - 1.0
    q11 = jnp.where(is_last, mu * m1 - 1.0, mu * mu - 1.0) * recip
    q12 = jnp.where(is_last, m1, mu) * recip
    q13 = recip
    q22 = jnp.where(is_last, mu * m1, mu * mu) * recip
    q23 = mu * recip
    q33 = (mu * mu - 1.0) * recip
    return q11, q12, q13, q22, q23, q33


def thirds(x):
    high = x.astype(bf16)
    rest = x - high.astype(f32)
    middle = rest.astype(bf16)
    return high, middle, (rest - middle.astype(f32)).astype(bf16)


def remote(src, dst, send_sem, recv_sem, to):
    return pltpu.make_async_remote_copy(
        src_ref=src,
        dst_ref=dst,
        send_sem=send_sem,
        recv_sem=recv_sem,
        device_id=to,
        device_id_type=pl.DeviceIdType.MESH,
    )


def stage_kernel(second, *refs):
    refs = list(refs)
    idx_ref = refs.pop(0)
    if second:
        own, other, vin, old, by_b, byd_b, bx_b, bxd_b = refs[:8]
        refs = refs[8:]
    else:
        raw = refs.pop(0)
    tables = refs[:8]
    vout, keep, recv = refs[8:11]
    refs = refs[11:]
    if second:
        now, sent, press = refs[:3]
        raw = sent
        refs = refs[3:]
    else:
        now, pivots, sent = refs[:3]
        local_tables = refs[3:11]
        load_sem = refs[11]
        refs = refs[12:]
        loads = [pltpu.make_async_copy(raw, sent, load_sem.at[0])]
        for i, (source, target) in enumerate(zip(tables, local_tables)):
            loads.append(pltpu.make_async_copy(source, target, load_sem.at[i + 1]))
        for load in loads:
            load.start()
        tables = local_tables
    mask, visc, dlx, dly, by, byd, bx, bxd = tables
    part, halo, spec, work, frp, fr, side, pick, covered, hs, hr, fs, fr_sem, xs, xr = refs
    _, _, nx, ny = now.shape
    fringe = fr.shape[2]
    sec = lax.axis_index("sec")
    me = lax.axis_index("gz")
    slabs = lax.axis_size("gz")
    is_farm = sec == 1
    core = lax.rem(me, 2)
    half = nx // 2
    has_below = (me > 0).astype(f32)
    has_above = (me < slabs - 1).astype(f32)

    out_level, in_level = core, 1 - core
    far = lax.rem(me + 2 * core - 1 + slabs, slabs)
    near = me + 1 - 2 * core
    has_far = jnp.where(core == 0, has_below, has_above)
    lid = jnp.where(core == 0, 1.0, has_above).astype(f32)

    barrier = pltpu.get_barrier_semaphore()
    for to in (
        {"sec": sec, "gz": far},
        {"sec": sec, "gz": near},
        {"sec": 1 - sec, "gz": me},
        {"sec": 1 - sec, "gz": far},
    ):
        pl.semaphore_signal(
            barrier, inc=1, device_id=to, device_id_type=pl.DeviceIdType.MESH
        )

    def far_face(c):
        to = {"sec": sec, "gz": far}
        return remote(raw.at[c, out_level], halo.at[0, c], hs.at[0, c], hr.at[0, c], to)

    def near_face(c):
        to = {"sec": sec, "gz": near}
        return remote(now.at[c, in_level], halo.at[1, c], hs.at[1, c], hr.at[1, c], to)

    def columns(i):
        farm = 1 - sec
        if i == 0:
            return remote(frp, fr, fs.at[0], fr_sem.at[0], {"sec": farm, "gz": me})
        return remote(frp.at[out_level], side, fs.at[1], fr_sem.at[1], {"sec": farm, "gz": far})

    def trade(field):
        rows = pl.ds(pl.multiple_of((1 - core) * half, half), half)
        to = {"sec": sec, "gz": near}
        return remote(spec.at[field, rows, :], recv.at[field], xs.at[field], xr.at[field], to)

    def project(c, z):
        p = press[z]
        if c == 0:
            raw[c, z] = vin[c, z] - right3(back3(bxd_b, p), by_b)
        elif c == 1:
            raw[c, z] = vin[c, z] - right3(back3(bx_b, p), byd_b)
        else:
            raw[c, z] = vin[c, z] - right3(back3(bx_b, press[z + 1] - p), by_b)

    order = (2, 1, 0)
    if second:
        press[:, pl.ds(pl.multiple_of(core * half, half), half), :] = own[...]
        press[:, pl.ds(pl.multiple_of((1 - core) * half, half), half), :] = other[...]
        project(order[0], out_level)
    pl.semaphore_wait(barrier, 4)
    far_face(order[0]).start()
    if second:
        project(order[1], out_level)
        project(order[2], out_level)

        @pl.when(is_farm)
        def _():
            far_face(order[1]).start()
            far_face(order[2]).start()

        for c in order:
            project(c, in_level)

    if not second:
        loads[0].wait()

    @pl.when(jnp.logical_not(is_farm))
    def _():
        place = lax.broadcasted_iota(jnp.int32, (fringe, 1), 0)
        tall = jnp.full((fringe, 1), -1, jnp.int32)
        for f in range(fringe):
            tall = jnp.where(place == f, idx_ref[f], tall)
        hit = lax.broadcasted_iota(jnp.int32, (fringe, nx), 1) == tall
        hit = hit.astype(f32).astype(bf16)
        for z in range(2):
            for c in range(3):
                high, middle, low = thirds(sent[c, z])
                frp[z, c] = (dot(hit, high) + dot(hit, middle)) + dot(hit, low)
        columns(0).start()
        columns(1).start()
        if second:
            far_face(order[1]).start()
            far_face(order[2]).start()

    if not second:
        for c in order[1:]:
            far_face(c).start()
        pivot_table(nx, ny, slabs // 2, pivots)

    def placed(rows, here):
        high, middle, low = thirds(rows)
        stack = jnp.concatenate([high, middle, low, jnp.zeros_like(low)], axis=0)
        return jnp.where(covered[...] > 0.5, dot(pick[...], stack), here)

    @pl.when(is_farm)
    def _():
        lane = lax.broadcasted_iota(jnp.int32, (1, 4 * fringe), 1)
        wide = jnp.full((1, 4 * fringe), -1, jnp.int32)
        for f in range(fringe):
            here = (lane == f) | (lane == f + fringe) | (lane == f + 2 * fringe)
            wide = jnp.where(here, idx_ref[f], wide)
        hit = lax.broadcasted_iota(jnp.int32, (nx, 4 * fringe), 0) == wide
        pick[...] = hit.astype(f32).astype(bf16)
        ones = jnp.ones((fringe, ny), f32)
        ones = jnp.concatenate([ones, jnp.zeros((3 * fringe, ny), f32)], axis=0)
        covered[...] = dot(pick[...], ones.astype(bf16))
        columns(0).wait_recv()
        for z in range(2):
            for c in range(3):
                now[c, z] = placed(fr[z, c], sent[c, z])

    @pl.when(jnp.logical_not(is_farm))
    def _():
        now[...] = sent[...]

    for c in order:
        near_face(c).start()

    if not second:
        for load in loads[1:]:
            load.wait()
    coef = jnp.where(is_farm, drag_coef, 0.0).astype(f32)
    for z in range(2):
        u = now[0, z]
        v = now[1, z]
        drag = coef * mask[z].astype(f32) * jnp.abs(u)
        for c in range(3):
            here = now[c, z]
            r = here.astype(bf16)
            part[c, z] = -(u * dot(dlx[...], r) + v * dot(r, dly[...])) - drag * here

    def update(c, z, beyond, edge):
        here = now[c, z]
        inner = now[c, 1 - z]
        side_sign = (2 * z - 1).astype(f32)
        tend = part[c, z] - now[2, z] * ((0.5 * side_sign) * (beyond - inner))
        tend = tend + visc[z] * (beyond - 2.0 * here + inner)
        if second:
            new = 0.5 * (old[c, z] + here + step_size * tend)
        else:
            new = here + step_size * tend
        if c == 2 and edge:
            new = new * lid
        vout[c, z] = new
        return new

    for c in order:
        near_face(c).wait_recv()
        new = update(c, in_level, halo[1, c], False)
        if c == 2:
            work[1] = right3(new, by)
        elif c == 1:
            spec[in_level] = right3(new, byd)
        else:
            spec[2] = right3(new, by)

    @pl.when(is_farm)
    def _():
        columns(1).wait_recv()

    for c in order:
        far_face(c).wait_recv()

        @pl.when(is_farm)
        def _():
            work[0] = placed(side[c], halo[0, c])

        @pl.when(jnp.logical_not(is_farm))
        def _():
            work[0] = halo[0, c]

        new = update(c, out_level, work[0] * has_far, True)
        if c == 2:
            w_out = right3(new, by)
            w_in = work[1]
            spec[out_level] = w_out - jnp.where(core == 1, w_in, 0.0)
            w_in = w_in - jnp.where(core == 0, w_out, 0.0)
            spec[in_level] = fore3(bx, spec[in_level] + w_in) + fore3(bxd, spec[2])
            trade(in_level).start()
            spec[2] = fore3(bx, jnp.where(core == 0, work[1], w_out))
            trade(2).start()
        elif c == 1:
            spec[out_level] = fore3(bx, spec[out_level] + right3(new, byd))
        else:
            spec[out_level] = spec[out_level] + fore3(bxd, right3(new, by))
            trade(out_level).start()
    keep[...] = spec[:, pl.ds(pl.multiple_of(core * half, half), half), :]
    for field in range(3):
        trade(field).wait()
    for c in range(3):
        far_face(c).wait_send()
        near_face(c).wait_send()

    @pl.when(jnp.logical_not(is_farm))
    def _():
        columns(0).wait_send()
        columns(1).wait_send()


def sources(core, keep, recv, rows):
    first = core == 0

    def pick(field, low):
        own, other = keep[field, rows, :], recv[field, rows, :]
        return jnp.where(first == low, own, other)

    s1 = pick(1, True)
    s2 = pick(0, False) - pick(2, True)
    s3 = pick(1, False)
    return pick, s1, s2, s3


def own_gap(h, nx, ny):
    me = lax.axis_index("gz")
    core = lax.rem(me, 2)
    chip = lax.div(me, 2)
    lane_blocks = ny // 128
    place = lax.broadcasted_iota(jnp.int32, (8, 128), 0)
    place = jnp.where(place < 4, place, place - 4)
    a = core * (nx // 2) + lax.div(chip, lane_blocks) * 8 + 4 * h + place
    b = lax.rem(chip, lane_blocks) * 128 + lax.broadcasted_iota(jnp.int32, (8, 128), 1)
    return parity_gap(a, nx) + wave_gap(b, ny)


def pivot_table(nx, ny, chips, pivots):
    for h in range(2):
        eps = own_gap(h, nx, ny)
        mu = 2.0 + eps
        mm = mu * mu
        inner = mm * eps * (4.0 + eps)
        lid = mm * (mu - 1.0) - 2.0 * mu + 1.0
        last = mu * eps * (mm * mm * (mu + 1.0) - mm * (4.0 * mu + 3.0) + 3.0 * mu + 1.0) / lid
        e = mu * eps * (mm + mu - 1.0)
        pivot = 1.0 / (1.0 + e)
        pivots[h, 0] = pivot

        def body(j, carry):
            e, pivot = carry
            e = inner + e * pivot
            pivot = 1.0 / (1.0 + e)
            pivots[h, j] = pivot
            return e, pivot

        e, pivot = lax.fori_loop(1, chips - 1, body, (e, pivot))
        e = last + e * pivot
        pivots[h, chips - 1] = jnp.where(e > 0.0, 1.0 / jnp.where(e > 0.0, e, 1.0), 0.0)


def solve_kernel(
    nx, ny, chips, keep, recv, pivots, own, other, fore, fore_in, back, back_in, work, out, ss, rs
):
    me = lax.axis_index("gz")
    core = lax.rem(me, 2)
    chip = lax.div(me, 2)
    is_last = chip == chips - 1
    half = keep.shape[1]
    lane_blocks = ny // 128
    row_blocks = half // 8
    pieces = 4
    mesh_id = pl.DeviceIdType.MESH
    sibling = {"gz": chip * 2 + (1 - core)}

    def peer(d):
        return {"gz": d * 2 + core}

    def push(src, dst, lane, to):
        return remote(src, dst, ss.at[lane], rs.at[lane], to)

    barrier = pltpu.get_barrier_semaphore()
    pl.semaphore_signal(barrier, inc=1, device_id=sibling, device_id_type=mesh_id)

    def greet(s, carry):
        to = peer(lax.rem(chip + s, chips))
        pl.semaphore_signal(barrier, inc=1, device_id=to, device_id_type=mesh_id)
        return carry

    lax.fori_loop(1, chips, greet, 0)

    def reduce(s, carry):
        rb = lax.rem(lax.div(chip, lane_blocks) + s, row_blocks)
        rows = pl.ds(pl.multiple_of(rb * 8, 8), 8)
        pick, s1, s2, s3 = sources(core, keep, recv, rows)
        mu = 2.0 + tile_gap(core * half + rb * 8, 0, 8, ny, nx, ny)
        q11, q12, q13, q22, q23, q33 = interior_inverse(mu, is_last)
        a = -pick(0, True) - (q11 * s1 + q12 * s2 + q13 * s3)
        c = pick(2, False) - (q13 * s1 + q23 * s2 + q33 * s3)
        for lb in range(lane_blocks):
            lanes = slice(lb * 128, (lb + 1) * 128)
            for h in range(2):
                rows4 = slice(4 * h, 4 * h + 4)
                pair = [a[rows4, lanes], c[rows4, lanes]]
                fore[h, rb * lane_blocks + lb] = jnp.concatenate(pair, axis=0)
        return carry

    lax.fori_loop(0, row_blocks, reduce, 0)
    pl.semaphore_wait(barrier, chips)

    def scatter(source, target, lane):
        def send(s, carry):
            d = lax.rem(chip + s, chips)
            push(source.at[d], target.at[chip], lane, peer(d)).start()
            return carry

        lax.fori_loop(1, chips, send, 0)
        target[chip] = source[chip]
        most = pl.ds(0, chips - 1)
        return push(source.at[most], target.at[most], lane, sibling)

    low = lax.broadcasted_iota(jnp.int32, (8, 128), 0) < 4

    def column(h):
        mu = 2.0 + own_gap(h, nx, ny)
        det = mu * (mu * mu - 2.0)
        tile = fore_in[h, 0]
        turned = pltpu.roll(tile, 4, 0)
        y = det * jnp.where(low, tile, turned) * pivots[h, 0]
        work[0] = y
        for j in range(1, chips):
            carry = jnp.where(low, turned, tile)
            tile = fore_in[h, j]
            turned = pltpu.roll(tile, 4, 0)
            y = (det * (jnp.where(low, tile, turned) + carry) + y) * pivots[h, j]
            work[j] = y
        back[h, chips - 1] = jnp.where(low, y, 0.0)
        for j in range(chips - 2, -1, -1):
            above = y
            y = work[j] + y * pivots[h, j]
            back[h, j] = jnp.where(low, y, above)

    trips = [scatter(fore.at[h], fore_in.at[h], 1 + h) for h in range(2)]
    for h in range(2):
        trips[h].wait_recv()
        column(h)
        trips.append(scatter(back.at[h], back_in.at[h], 3 + h))
    for h in range(2):
        trips[2 + h].wait_recv()

    def expand(rb, carry):
        rows = pl.ds(pl.multiple_of(rb * 8, 8), 8)
        _, s1, s2, s3 = sources(core, keep, recv, rows)
        mu = 2.0 + tile_gap(core * half + rb * 8, 0, 8, ny, nx, ny)
        q11, q12, q13, q22, q23, q33 = interior_inverse(mu, is_last)
        cols = range(lane_blocks)
        top = jnp.concatenate([back_in[0, rb * lane_blocks + lb] for lb in cols], axis=1)
        bottom = jnp.concatenate([back_in[1, rb * lane_blocks + lb] for lb in cols], axis=1)
        p0 = jnp.concatenate([top[:4], bottom[:4]], axis=0)
        p4 = jnp.concatenate([top[4:], bottom[4:]], axis=0)
        s1 = s1 - p0
        s3 = s3 - p4
        p1 = -(q11 * s1 + q12 * s2 + q13 * s3)
        p2 = -(q12 * s1 + q22 * s2 + q23 * s3)
        p3 = -(q13 * s1 + q23 * s2 + q33 * s3)
        p4 = jnp.where(is_last, p3, p4)
        first = core == 0
        for field, (low, high) in enumerate(((p0, p2), (p1, p3), (p2, p4))):
            own[field, rows, :] = jnp.where(first, low, high)
            out[field, rows, :] = jnp.where(first, high, low)
        return carry

    step = row_blocks // pieces
    for piece in range(pieces):
        lax.fori_loop(piece * step, (piece + 1) * step, expand, 0)
        rows = pl.ds(piece * step * 8, step * 8)
        push(out.at[:, rows, :], other.at[:, rows, :], 0, sibling).start()
    push(out, other, 0, sibling).wait()
    for trip in trips:
        trip.wait_send()


def backward_kernel(own, other, vin, by, byd, bx, bxd, out, press, new, sems):
    half = own.shape[1]
    core = lax.rem(lax.axis_index("gz"), 2)
    press[:, pl.ds(pl.multiple_of(core * half, half), half), :] = own[...]
    press[:, pl.ds(pl.multiple_of((1 - core) * half, half), half), :] = other[...]
    copies = []

    def finish(c, z, correction):
        new[c, z] = vin[c, z] - correction
        copies.append(pltpu.make_async_copy(new.at[c, z], out.at[c, z], sems.at[c, z]))
        copies[-1].start()

    for z in range(2):
        p = press[z]
        lift = press[z + 1] - p
        finish(0, z, right3(back3(bxd, p), by))
        finish(1, z, right3(back3(bx, p), byd))
        finish(2, z, right3(back3(bx, lift), by))
    for copy in copies:
        copy.wait()


VM = pl.BlockSpec(memory_space=pltpu.VMEM)
SM = pl.BlockSpec(memory_space=pltpu.SMEM)
HB = pl.BlockSpec(memory_space=pltpu.HBM)


def shape(*dims):
    return jax.ShapeDtypeStruct(dims, f32)


def call(kernel, ins, outs, scratch=(), limit=40, flops=0, collective=None, specs=None, to=VM):
    many = isinstance(outs, (list, tuple))
    moved = sum(x.size * x.dtype.itemsize for x in ins)
    moved += sum(math.prod(o.shape) * 4 for o in (outs if many else [outs]))
    return pl.pallas_call(
        kernel,
        out_shape=outs,
        in_specs=specs or [VM] * len(ins),
        out_specs=[to] * len(outs) if many else to,
        scratch_shapes=[pltpu.VMEM(s, f32) if isinstance(s, tuple) else s for s in scratch],
        compiler_params=pltpu.CompilerParams(
            vmem_limit_bytes=limit * MIB,
            collective_id=collective,
            has_side_effects=collective is not None,
        ),
        cost_estimate=pl.CostEstimate(flops=flops, bytes_accessed=moved, transcendentals=0),
    )(*ins)


def local(velocity, eddy_viscosity, turbine_mask, idx):
    velocity = velocity[0]
    visc = eddy_viscosity[0]
    _, _, nx, ny = velocity.shape
    fringe = idx.shape[0]
    slabs = lax.axis_size("gz")
    chips = slabs // 2
    half = nx // 2
    plane = 2 * nx * ny

    slope_x, slope_y = by_parity(basis_slope_np(nx)), basis_slope_np(ny)
    base_x, base_y = by_parity(basis_np(nx)), basis_np(ny)
    turned = (0, 2, 1)
    dlx = jnp.asarray(derivative_np(nx, (nx - 1) // 3).astype(np.float32).astype(bf16))
    dly = jnp.asarray(derivative_np(ny, (ny - 1) // 3).T.astype(np.float32).astype(bf16))
    fore = [hi_lo(base_y.T), hi_lo(slope_y.T), stacked(base_x), stacked(slope_x)]
    back = [
        hi_lo(base_y),
        hi_lo(-slope_y),
        stacked(base_x.transpose(turned)),
        stacked(-slope_x.transpose(turned)),
    ]
    fore = [jnp.asarray(t) for t in fore]
    back = [jnp.asarray(t) for t in back]
    field = (3, 2, nx, ny)
    dma = pltpu.SemaphoreType.DMA
    stage_out = [shape(*field), shape(3, half, ny), shape(3, half, ny)]
    stage_scratch = [
        field,
        (2, 3, nx, ny),
        (3, nx, ny),
        (2, nx, ny),
        (2, 3, fringe, ny),
        (2, 3, fringe, ny),
        (3, fringe, ny),
        pltpu.VMEM((nx, 4 * fringe), bf16),
        (nx, ny),
        dma((2, 3)),
        dma((2, 3)),
        dma((2,)),
        dma((2,)),
        dma((3,)),
        dma((3,)),
    ]
    shared = [turbine_mask, visc, dlx, dly] + fore
    ahead = plane * (6 * nx + 6 * ny) + 3 * plane * (6 * ny + 5 * nx)

    def solve(keep, recv, pivots):
        column = (2, chips, 8, 128)
        return call(
            functools.partial(solve_kernel, nx, ny, chips),
            [keep, recv, pivots],
            [shape(3, half, ny), shape(3, half, ny)],
            scratch=[column] * 4 + [(chips, 8, 128), (3, half, ny)] + [dma((5,))] * 2,
            limit=12,
            collective=0,
        )

    loaded = [field] + [pltpu.VMEM(t.shape, t.dtype) for t in shared] + [dma((9,))]
    state, keep, recv, start, pivots = call(
        functools.partial(stage_kernel, False),
        [idx] + [pltpu.with_memory_space_constraint(x, pltpu.HBM) for x in [velocity] + shared],
        stage_out + [shape(*field), shape(2, chips, 8, 128)],
        scratch=loaded + stage_scratch,
        limit=30,
        flops=ahead,
        collective=1,
        specs=[SM] + [HB] * (1 + len(shared)),
    )
    own, other = solve(keep, recv, pivots)
    state, keep, recv = call(
        functools.partial(stage_kernel, True),
        [idx, own, other, state, start] + back + shared,
        stage_out,
        scratch=[field, field, (3, nx, ny)] + stage_scratch,
        limit=28,
        flops=ahead + 3 * plane * (6 * ny + 6 * nx),
        collective=2,
        specs=[SM] + [VM] * (8 + len(shared)),
    )
    own, other = solve(keep, recv, pivots)
    result = call(
        backward_kernel,
        [own, other, state] + back,
        shape(*field),
        scratch=[(3, nx, ny), field, dma((3, 2))],
        limit=16,
        flops=3 * plane * (6 * ny + 6 * nx),
        to=HB,
    )
    return result[None]


def solution(mesh):
    placed = (
        P("sec", None, "gz", None, None),
        P("sec", "gz", None, None),
        P("gz", None, None),
        P(),
    )
    return jax.shard_map(
        local,
        mesh=mesh,
        in_specs=placed,
        out_specs=P("sec", None, "gz", None, None),
        check_vma=False,
    )
```
